1024 devices in a mesh: exp: 32 (over x, y), seq: 32 (over z, core).
Axes of the slice: x: 4, y: 8, z: 16, core: 2. Of those that a mesh axis runs over, the one named last changes fastest.
Arguments:
- output_gradient: bfloat16 [4096, 4096], P('exp', 'seq'), may hold values from -6 to 6
- routed_expert_index: int32 [4096, 8], P('exp'), may hold values from 0 to 127, all different within a row; in each aligned block of 128 rows (0 to 127, 128 to 255, ...) at most 12 rows name the same one
- combine: bfloat16 [4096, 8], P('exp'), may hold values from 0.049804688 to 0.5
- token_task_index: int32 [4096], P('exp'), may hold values from 0 to 7
- saved_gate_input: bfloat16 [128, 32, 12, 1536], P('exp', None, None, 'seq'), may hold values from -6 to 6
- saved_up_input: bfloat16 [128, 32, 12, 1536], P('exp', None, None, 'seq'), may hold values from -6 to 6
- down_weight: bfloat16 [128, 1536, 4096], P('exp', None, 'seq'), may hold values from -0.15625 to 0.15625
- adapter_first_factor: bfloat16 [128, 8, 1536, 64], P('exp', None, 'seq'), may hold values from -0.15625 to 0.15625
- adapter_second_factor: bfloat16 [128, 8, 64, 4096], P('exp', None, None, 'seq'), may hold values from -0.1875 to 0.1875
Outputs:
- grad_gate_pre: bfloat16 [128, 32, 12, 1536], P('exp', None, None, 'seq')
- grad_up_pre: bfloat16 [128, 32, 12, 1536], P('exp', None, None, 'seq')
- grad_lora_a: bfloat16 [128, 8, 1536, 64], P('exp', None, 'seq')
- grad_lora_b: bfloat16 [128, 8, 64, 4096], P('exp', None, None, 'seq')
- grad_combine: float32 [4096, 8], P('exp')
The draws below stay inside these ranges and needn't reach their ends.
Inputs may be any that keep to these rules, and one draw needn't show every extreme that they name: `routed_expert_index`: each token names 8 different experts; among the tokens of one exp index (aligned blocks of 128 tokens) no expert is named more than 12 times, a bound that some block reaches.
All inputs are finite; a program needn't handle non-finite values.
Results may differ from the reference program's by a relative error of at most 0.015.
Values may be sent and summed in bfloat16 or wider, within the bound.
No kernel may reach another device: no remote copies, remote signals or barrier semaphores. Data moves between devices by JAX's collectives and lax.ppermute only.
A program may use at most 128 MiB of HBM per device.

```python
import math
from functools import partial
import jax
import jax.numpy as jnp
import numpy as np
from jax import lax

MODEL_WIDTH = 4096
HIDDEN_UNITS = 1536
TOP = 8
ADAPTER_RANK = 64
TASK_TOTAL = 8
MOST = 12
TOK_DEV = 128
TOKENS = 4096
EXPERT_TOTAL = 128
N_EXP = 32


def plant(array, stream_key, smallest, top_value):
    longest = array.shape.index(max(array.shape))
    spots = []
    for shift in (0, 1):
        where = [jax.random.randint(jax.random.fold_in(stream_key, axis), (), 0, length) for axis, length in enumerate(array.shape)]
        where[longest] = (where[longest] + shift) % array.shape[longest]
        spots.append(tuple(where))
    return array.at[spots[0]].set(smallest).at[spots[1]].set(top_value)


def level_of(rng, shape, cuts, least, largest):
    def one(position, blocks):
        draws = jax.random.uniform(jax.random.fold_in(jax.random.fold_in(rng, 6), position), (blocks,), jnp.float32, least / len(cuts), largest / len(cuts))
        return jnp.repeat(jnp.exp(draws), shape[position] // blocks).reshape((-1,) + (1,) * (len(shape) - position - 1))

    gain = one(*cuts[0])
    for cut in cuts[1:]:
        gain = gain * one(*cut)
    return gain


def deal_out(own_key, own, number, rows, amount, top, bound, skew):
    ranking = jax.random.permutation(own_key, amount)
    crowded, usual = load_shares(amount, rows * top, bound, skew, True), load_shares(amount, rows * top, bound, skew, False)
    places = jnp.arange(amount)

    def named(tallies, turn):
        used = int((tallies > 0).sum())
        fixed = max(1, used // 4)
        shifted = fixed + (places - fixed + turn * (used - fixed)) % max(1, amount - fixed)
        return jnp.zeros((amount,), jnp.int32).at[ranking[jnp.where(places < fixed, places, shifted)]].set(jnp.asarray(tallies, jnp.int32))

    tallies = jnp.where(number % 4 == 0, named(crowded, number // 4), named(usual, number - number // 4 - 1))
    mixed = jax.random.permutation(jax.random.fold_in(own, 3), amount)
    source_of, sink = mixed[0:amount // 2 * 2:2], mixed[1:amount // 2 * 2:2]
    margin = jnp.minimum(tallies[source_of] - 1, bound - tallies[sink]) // 2
    margin = jnp.where((source_of == ranking[0]) | (sink == ranking[0]) | (tallies[sink] == 0), 0, jnp.maximum(margin, 0))
    shifted = jax.random.randint(jax.random.fold_in(own, 4), (amount // 2,), 0, 1 << 20) % (margin + 1)
    tallies = tallies.at[source_of].add(-shifted).at[sink].add(shifted)
    labels = jnp.searchsorted(jnp.cumsum(tallies), jnp.arange(rows * top), side="right").astype(jnp.int32)
    listing = labels.reshape(top, rows).T
    listing = listing[jax.random.permutation(jax.random.fold_in(own, 1), rows)]
    turn = jax.random.randint(jax.random.fold_in(own, 2), (rows, 1), 0, top)
    return jnp.take_along_axis(listing, (jnp.arange(top)[None, :] + turn) % top, axis=1)


def load_shares(count, total, most, slope, full):
    loads = [(1 << 20) // math.isqrt(standing ** slope) + 1 for standing in range(1, count + 1)]
    largest = most if full else min(most, max(-(-total // count), total * loads[0] // sum(loads)))
    least = 1 if total - largest >= count - 1 else 0
    holding, spare = [largest] + [least] * (count - 1), total - largest - least * (count - 1)
    while spare > 0:
        movable = [i for i in range(1, count) if holding[i] < largest] or [i for i in range(1, count) if holding[i] < most]
        whole, remaining = sum([loads[i] for i in movable]), spare
        for i in movable:
            extra = min(most - holding[i], max(1, remaining * loads[i] // whole), spare)
            holding[i] = holding[i] + extra
            spare = spare - extra
    return np.array(holding)


def gaussian(stream_key, shape, spread, bound, pieces=(), kind=jnp.bfloat16):
    result = jax.random.normal(stream_key, shape, jnp.float32) * spread
    if len(pieces) > 0:
        result = level_of(stream_key, shape, pieces, -0.22, 0.18) * result
    return jnp.clip(result, min=-bound, max=bound).astype(kind)


def setup_inputs(seed: int = 0) -> dict:
    streams_of = jax.random.split(jax.random.key(seed), 10)
    output_gradient = gaussian(streams_of[0], (TOKENS, MODEL_WIDTH), 1.0, 6.0, ((0, 32), (1, 32)))
    routed_expert_index_keys = jax.random.split(jax.random.fold_in(streams_of[1], 1), TOKENS // TOK_DEV)
    routed_expert_index_turns = jax.random.permutation(jax.random.fold_in(streams_of[1], 3), TOKENS // TOK_DEV)
    routed_expert_index = jax.vmap(lambda own, number: deal_out(jax.random.fold_in(streams_of[1], 2), own, number, TOK_DEV, EXPERT_TOTAL, TOP, MOST, 2))(routed_expert_index_keys, routed_expert_index_turns).reshape((TOKENS, TOP))
    combine = jnp.clip(0.049804688 + 0.4501953 * jax.random.uniform(streams_of[2], (TOKENS, TOP), jnp.float32) ** level_of(streams_of[2], (TOKENS, TOP), ((0, 32),), -0.2, 0.2), 0.049804688, 0.5).astype(jnp.bfloat16)
    token_task_index = plant(jax.random.randint(streams_of[3], (TOKENS,), 0, TASK_TOTAL), jax.random.fold_in(streams_of[3], 1), 0, TASK_TOTAL - 1).astype(jnp.int32)
    saved_gate_input = gaussian(streams_of[4], (EXPERT_TOTAL, N_EXP, MOST, HIDDEN_UNITS), 1.0, 6.0, ((0, 32), (3, 32)))
    saved_up_input = gaussian(streams_of[5], (EXPERT_TOTAL, N_EXP, MOST, HIDDEN_UNITS), 1.0, 6.0, ((0, 32), (3, 32)))
    down_weight = gaussian(streams_of[6], (EXPERT_TOTAL, HIDDEN_UNITS, MODEL_WIDTH), HIDDEN_UNITS ** -0.5, 0.15625, ((0, 32), (2, 32)))
    adapter_first_factor = gaussian(streams_of[7], (EXPERT_TOTAL, TASK_TOTAL, HIDDEN_UNITS, ADAPTER_RANK), HIDDEN_UNITS ** -0.5, 0.15625, ((0, 32), (2, 32)))
    adapter_second_factor = gaussian(streams_of[8], (EXPERT_TOTAL, TASK_TOTAL, ADAPTER_RANK, MODEL_WIDTH), (MODEL_WIDTH // 4) ** -0.5, 0.1875, ((0, 32), (3, 32)))
    return {"output_gradient": output_gradient, "routed_expert_index": routed_expert_index, "combine": combine, "token_task_index": token_task_index, "saved_gate_input": saved_gate_input, "saved_up_input": saved_up_input, "down_weight": down_weight, "adapter_first_factor": adapter_first_factor, "adapter_second_factor": adapter_second_factor}


def per_expert_update(out_grad_all, operands):
    gate_in, up_in, down_mat, factor_a, factor_b, token_idx, gate_activated, task_idx = operands
    token_rows = out_grad_all[token_idx.reshape(-1)]
    gate_activated = gate_activated.reshape(-1)
    task_idx = task_idx.reshape(-1)
    gate_f = gate_in.reshape(-1, HIDDEN_UNITS).astype(jnp.float32)
    up_f = up_in.reshape(-1, HIDDEN_UNITS).astype(jnp.float32)
    sigmoid_gate = jax.nn.sigmoid(gate_f)
    activation = gate_f * sigmoid_gate
    hidden_state = (activation * up_f).astype(jnp.bfloat16)
    task_mask = (task_idx[:, None] == jnp.arange(TASK_TOTAL, dtype=jnp.int32)[None, :]).astype(jnp.float32)
    latent_rows_full = jnp.einsum('sf,tfr->str', hidden_state.astype(jnp.float32), factor_a.astype(jnp.float32))
    latent = jnp.sum(latent_rows_full * task_mask[:, :, None], axis=1).astype(jnp.bfloat16)
    back_hidden = jnp.dot(token_rows, down_mat.T, preferred_element_type=jnp.float32)
    rows_f = token_rows.astype(jnp.float32)
    query_latent_full = jnp.einsum('sd,trd->str', rows_f, factor_b.astype(jnp.float32))
    query_lat = jnp.sum(query_latent_full * task_mask[:, :, None], axis=1)
    down_weight_gradient = jnp.sum(hidden_state.astype(jnp.float32) * back_hidden, axis=1) + jnp.sum(latent.astype(jnp.float32) * query_lat, axis=1)
    scaled_lat = (gate_activated[:, None] * query_lat).astype(jnp.bfloat16)
    spread_update = task_mask[:, :, None] * scaled_lat.astype(jnp.float32)[:, None, :]
    hidden_grad = gate_activated[:, None] * back_hidden + jnp.einsum('str,tfr->sf', spread_update, factor_a.astype(jnp.float32))
    gate_input_gradient = (hidden_grad * up_f * sigmoid_gate * (1.0 + gate_f * (1.0 - sigmoid_gate))).astype(jnp.bfloat16)
    up_input_gradient = (hidden_grad * activation).astype(jnp.bfloat16)
    first_factor_gradient = jnp.einsum('str,sf->tfr', spread_update, hidden_state.astype(jnp.float32)).astype(jnp.bfloat16)
    weighted_lat = (gate_activated[:, None] * latent.astype(jnp.float32)).astype(jnp.bfloat16)
    spread_z = task_mask[:, :, None] * weighted_lat.astype(jnp.float32)[:, None, :]
    second_factor_gradient = jnp.einsum('str,sd->trd', spread_z, rows_f).astype(jnp.bfloat16)
    return (gate_input_gradient.reshape(N_EXP, MOST, HIDDEN_UNITS), up_input_gradient.reshape(N_EXP, MOST, HIDDEN_UNITS), first_factor_gradient, second_factor_gradient, down_weight_gradient.reshape(N_EXP, MOST))


def reference(output_gradient, routed_expert_index, combine, token_task_index, saved_gate_input, saved_up_input, down_weight, adapter_first_factor, adapter_second_factor):
    global_rows = TOK_DEV * TOP
    flat_ids = routed_expert_index.reshape(N_EXP, global_rows).astype(jnp.int32)
    onehot = (flat_ids[:, :, None] == jnp.arange(EXPERT_TOTAL, dtype=jnp.int32)[None, None, :]).astype(jnp.int32)
    before = jnp.cumsum(onehot, axis=1) - onehot
    place_rank = jnp.sum(before * onehot, axis=2).astype(jnp.int32)
    source_idx = jnp.broadcast_to(jnp.arange(N_EXP, dtype=jnp.int32)[:, None], (N_EXP, global_rows))
    within_idx = jnp.broadcast_to(jnp.arange(global_rows, dtype=jnp.int32)[None, :], (N_EXP, global_rows))
    base_table = jnp.zeros((EXPERT_TOTAL, N_EXP, MOST), jnp.int32)
    row_token_index = base_table.at[flat_ids, source_idx, place_rank].set((source_idx * TOK_DEV + within_idx // TOP).astype(jnp.int32))
    choice_of = base_table.at[flat_ids, source_idx, place_rank].set((within_idx % TOP).astype(jnp.int32))
    filled = jnp.zeros((EXPERT_TOTAL, N_EXP, MOST), jnp.float32).at[flat_ids, source_idx, place_rank].set(1.0)
    gate_activated = combine.astype(jnp.float32)[row_token_index, choice_of] * filled
    row_task_index = token_task_index[row_token_index]
    gate_input_gradient, up_input_gradient, first_factor_gradient, second_factor_gradient, down_weight_gradient = lax.map(partial(per_expert_update, output_gradient), (saved_gate_input, saved_up_input, down_weight, adapter_first_factor, adapter_second_factor, row_token_index, gate_activated, row_task_index))
    grad_combine = jnp.zeros((TOKENS, TOP), jnp.float32).at[row_token_index, choice_of].add(down_weight_gradient * filled)
    return (gate_input_gradient, up_input_gradient, first_factor_gradient, second_factor_gradient, grad_combine)
```

```python
import jax
import jax.numpy as jnp
from jax import lax
from jax.experimental import pallas as pl
from jax.experimental.pallas import tpu as pltpu
from jax.sharding import Mesh
from jax.sharding import PartitionSpec as P

BF = jnp.bfloat16
F32 = jnp.float32


def back_partial(core, weight, weight_peer, rows, rows_peer):
    exp_local, z_width, _, piece, width = weight.shape
    slots = rows.shape[1]

    def kernel(core_ref, w_ref, wp_ref, x_ref, xp_ref, out_ref):
        nums = (((1,), (1,)), ((), ()))
        own = w_ref[0, :, 0].reshape(z_width * piece, width)
        peer = wp_ref[0].reshape(z_width * piece, width)
        total = lax.dot_general(own, x_ref[0], nums, preferred_element_type=F32)
        total += lax.dot_general(peer, xp_ref[0], nums, preferred_element_type=F32)
        out_ref[:, 0] = total.astype(BF).reshape(z_width, piece, slots)

    return pl.pallas_call(
        kernel,
        out_shape=jax.ShapeDtypeStruct((z_width, exp_local, piece, slots), BF),
        grid_spec=pltpu.PrefetchScalarGridSpec(
            num_scalar_prefetch=1,
            grid=(exp_local,),
            in_specs=[
                pl.BlockSpec((1, z_width, 1, piece, width), lambda e, c: (e, 0, c[0], 0, 0)),
                pl.BlockSpec((1, z_width, piece, width), lambda e, c: (e, 0, 0, 0)),
                pl.BlockSpec((1, slots, width), lambda e, c: (e, 0, 0)),
                pl.BlockSpec((1, slots, width), lambda e, c: (e, 0, 0)),
            ],
            out_specs=pl.BlockSpec((z_width, 1, piece, slots), lambda e, c: (0, e, 0, 0)),
        ),
        name="back_partial",
    )(core.reshape(1), weight, weight_peer, rows, rows_peer)


def on_device(
    output_gradient,
    routed_expert_index,
    combine,
    token_task_index,
    saved_gate_input,
    saved_up_input,
    down_weight,
    adapter_first_factor,
    adapter_second_factor,
):
    exp_width = lax.axis_size("exp")
    z_width = lax.axis_size("z")
    core = lax.axis_index("core")
    z_index = lax.axis_index("z")
    exp_local, source_count, most, piece = saved_gate_input.shape
    tok_count, top = routed_expert_index.shape
    width = output_gradient.shape[1]
    task_count, rank = adapter_first_factor.shape[1], adapter_first_factor.shape[3]
    expert_count = exp_local * exp_width
    per_expert = source_count * most
    total_slots = exp_local * per_expert
    swap = [(0, 1), (1, 0)]

    weight = down_weight.reshape(exp_local, z_width, 2, piece, width)
    weight_peer = lax.ppermute(
        lax.dynamic_index_in_dim(weight, 1 - core, axis=2, keepdims=False), "core", swap
    )

    ids = routed_expert_index.T
    experts = jnp.arange(expert_count, dtype=jnp.int32)
    tokens = jnp.arange(tok_count, dtype=jnp.int32)
    names = ids[:, None, :] == experts[None, :, None]
    named = jnp.any(names, axis=0)
    gates = jnp.sum(jnp.where(names, combine.T[:, None, :].astype(F32), 0.0), axis=0)
    earlier = (tokens[:, None] < tokens[None, :]).astype(BF)
    place = jnp.dot(named.astype(BF), earlier, preferred_element_type=F32)
    place_or = jnp.where(named, place, -1.0).astype(BF)
    row_of = jnp.arange(expert_count * most, dtype=jnp.int32)
    spread = (row_of[:, None] // most == experts[None, :]).astype(BF)
    picked = jnp.dot(spread, place_or, preferred_element_type=F32) == (
        (row_of % most).astype(F32)[:, None]
    )
    send_rows = jnp.dot(picked.astype(BF), output_gradient, preferred_element_type=F32).astype(BF)
    slab = exp_local * most
    extra = -(exp_local + 1) % 8
    send = jnp.concatenate(
        [
            send_rows.reshape(exp_width, slab, width),
            gates.astype(BF).reshape(exp_width, exp_local, tok_count),
            jnp.broadcast_to(token_task_index.astype(BF), (exp_width, 1, tok_count)),
            jnp.zeros((exp_width, extra, tok_count), BF),
        ],
        axis=1,
    )
    received = lax.all_to_all(send, "exp", split_axis=0, concat_axis=0, tiled=True)

    rows = received[:, :slab].transpose(1, 0, 2).reshape(exp_local, per_expert, width)
    rows_peer = lax.ppermute(rows, "core", swap)
    gate_rows = received[:, slab : slab + exp_local].transpose(1, 0, 2)
    used = gate_rows > 0
    place_in = jnp.dot(
        used.astype(BF).reshape(exp_local * source_count, tok_count),
        earlier,
        preferred_element_type=F32,
    ).reshape(exp_local, source_count, tok_count)
    holds = used[:, None] & (
        place_in[:, None] == jnp.arange(most, dtype=jnp.int32).astype(F32)[:, None, None]
    )
    gate_slot = jnp.sum(jnp.where(holds, gate_rows.astype(F32)[:, None], 0.0), axis=3).reshape(
        exp_local, per_expert
    )
    task_rows = received[:, slab + exp_local].astype(F32)
    task_slot = jnp.sum(
        jnp.where(holds, task_rows, 0.0), axis=3
    ).reshape(exp_local, per_expert)
    task_mask = (
        task_slot[..., None] == jnp.arange(task_count, dtype=jnp.int32).astype(F32)
    ).astype(F32)

    partial = back_partial(core.astype(jnp.int32), weight, weight_peer, rows, rows_peer)
    back = lax.psum_scatter(partial, "z", scatter_dimension=0, tiled=True)[0]

    gate_f = saved_gate_input.swapaxes(1, 2).reshape(exp_local, per_expert, piece).astype(F32)
    up_f = saved_up_input.swapaxes(1, 2).reshape(exp_local, per_expert, piece).astype(F32)
    sig = jax.nn.sigmoid(gate_f)
    act = gate_f * sig
    hidden = (act * up_f).astype(BF)

    lat_all = jnp.einsum(
        "ujy,upyg->ujpg", hidden, adapter_first_factor, preferred_element_type=F32
    )
    lat_part = jnp.sum(lat_all * task_mask[..., None], axis=2)
    ql_all = jnp.einsum("akg,amqg->akmq", rows, adapter_second_factor, preferred_element_type=F32)
    ql_part = jnp.sum(ql_all * task_mask[..., None], axis=2)
    both = jnp.concatenate([lat_part, ql_part], axis=2).reshape(2, total_slots // 2, 2 * rank)
    theirs = lax.dynamic_index_in_dim(both, 1 - core, axis=0, keepdims=False)
    mine = lax.dynamic_index_in_dim(both, core, axis=0, keepdims=False)
    mine = mine + lax.ppermute(theirs.astype(BF), "core", swap).astype(F32)
    mine = mine.astype(BF).reshape(z_width, -1, 2 * rank)
    mine = lax.all_to_all(mine, "z", split_axis=0, concat_axis=0, tiled=True)
    mine = jnp.sum(mine.astype(F32), axis=0).astype(BF)
    half = lax.all_gather(mine, "z", axis=0, tiled=True)
    other = lax.ppermute(half, "core", swap)
    full = jnp.where(
        core == 0, jnp.concatenate([half, other]), jnp.concatenate([other, half])
    ).reshape(exp_local, per_expert, 2 * rank)
    back, full = lax.optimization_barrier((back, full))
    latent, query = full[..., :rank], full[..., rank:]
    query_f = query.astype(F32)

    scaled = (gate_slot[..., None] * query_f).astype(BF)
    spread_update = (task_mask[..., None] * scaled.astype(F32)[:, :, None, :]).astype(BF)
    weighted = (gate_slot[..., None] * latent.astype(F32)).astype(BF)
    spread_z = (task_mask[..., None] * weighted.astype(F32)[:, :, None, :]).astype(BF)
    first_grad = jnp.einsum(
        "estr,esf->etfr", spread_update, hidden, preferred_element_type=F32
    ).astype(BF)
    second_grad = jnp.einsum(
        "estr,esd->etrd", spread_z, rows, preferred_element_type=F32
    ).astype(BF)
    inner = jnp.sum(latent.astype(F32) * query_f, axis=2)
    update_part = jnp.einsum(
        "unqk,uqjk->unj", spread_update, adapter_first_factor, preferred_element_type=F32
    )

    back_f = jnp.swapaxes(back.astype(F32), 1, 2)
    first_device = (z_index == 0) & (core == 0)
    pair_part = jnp.sum(hidden.astype(F32) * back_f, axis=2) + jnp.where(first_device, inner, 0.0)
    dh = gate_slot[..., None] * back_f + update_part
    gate_grad = (dh * up_f * sig * (1.0 + gate_f * (1.0 - sig))).astype(BF)
    up_grad = (dh * act).astype(BF)

    returned = lax.all_to_all(
        pair_part.reshape(exp_local, most, source_count).transpose(2, 0, 1),
        "exp",
        split_axis=0,
        concat_axis=0,
        tiled=True,
    ).reshape(expert_count, most)
    finder = names.transpose(1, 0, 2).reshape(expert_count, top * tok_count).astype(BF)
    place_pick = jnp.sum(jnp.where(names, place[None], 0.0), axis=1).reshape(1, top * tok_count)
    found = jnp.dot(returned.astype(BF).T, finder, preferred_element_type=F32)
    found = jnp.sum(
        jnp.where(jnp.arange(most, dtype=jnp.int32).astype(F32)[:, None] == place_pick, found, 0.0),
        axis=0,
    ).reshape(top, tok_count)
    copies = jnp.broadcast_to(found.astype(BF), (z_width * 2, top, tok_count))
    pieces = lax.all_to_all(copies, ("z", "core"), split_axis=0, concat_axis=0, tiled=True)
    grad_combine = jnp.sum(pieces.astype(F32), axis=0).T
    shape_out = (exp_local, most, source_count, piece)
    return (
        gate_grad.reshape(shape_out).swapaxes(1, 2),
        up_grad.reshape(shape_out).swapaxes(1, 2),
        first_grad,
        second_grad,
        grad_combine,
    )


def solution(mesh):
    exp_width, seq_width = mesh.shape["exp"], mesh.shape["seq"]
    split = Mesh(mesh.devices.reshape(exp_width, seq_width // 2, 2), ("exp", "z", "core"))
    seq = ("z", "core")
    placed = (
        P("exp", seq),
        P("exp", None),
        P("exp", None),
        P("exp"),
        P("exp", None, None, seq),
        P("exp", None, None, seq),
        P("exp", None, seq),
        P("exp", None, seq, None),
        P("exp", None, None, seq),
    )
    return jax.shard_map(
        on_device,
        mesh=split,
        in_specs=placed,
        out_specs=(
            P("exp", None, None, seq),
            P("exp", None, None, seq),
            P("exp", None, seq, None),
            P("exp", None, None, seq),
            P("exp", None),
        ),
        check_vma=False,
    )
```

```python
import jax
import jax.numpy as jnp
from jax import lax
from jax.experimental import pallas as pl
from jax.experimental.pallas import tpu as pltpu
from jax.sharding import Mesh
from jax.sharding import PartitionSpec as P

BF = jnp.bfloat16
F32 = jnp.float32


def partial_sums(core, task_row, hidden, first, second, weight, weight_peer, rows, rows_peer):
    exp_local, z_width, _, piece, width = weight.shape
    slots = rows.shape[1]
    task_count, rank = first.shape[1], first.shape[3]
    more = 2 * rank // z_width

    def kernel(core_ref, t_ref, h_ref, a_ref, b_ref, w_ref, wp_ref, x_ref, xp_ref, out_ref):
        nums = (((1,), (1,)), ((), ()))
        x = x_ref[0]
        own = w_ref[0, :, 0].reshape(z_width * piece, width)
        peer = wp_ref[0].reshape(z_width * piece, width)
        total = lax.dot_general(own, x, nums, preferred_element_type=F32)
        total += lax.dot_general(peer, xp_ref[0], nums, preferred_element_type=F32)
        out_ref[:, :piece] = total.astype(BF).reshape(z_width, piece, slots)
        ql_all = lax.dot_general(
            b_ref[0].reshape(task_count * rank, width), x, nums, preferred_element_type=F32
        )
        lat = jnp.zeros((rank, slots), F32)
        ql = jnp.zeros((rank, slots), F32)
        for t in range(task_count):
            keep = t_ref[0] == float(t)
            part = lax.dot_general(
                a_ref[0, t], h_ref[0], (((0,), (0,)), ((), ())), preferred_element_type=F32
            )
            lat += jnp.where(keep, part, 0.0)
            ql += jnp.where(keep, ql_all[t * rank : (t + 1) * rank], 0.0)
        out_ref[: z_width // 2, piece:] = lat.astype(BF).reshape(z_width // 2, more, slots)
        out_ref[z_width // 2 :, piece:] = ql.astype(BF).reshape(z_width // 2, more, slots)

    return pl.pallas_call(
        kernel,
        out_shape=jax.ShapeDtypeStruct((z_width, piece + more, exp_local * slots), BF),
        grid_spec=pltpu.PrefetchScalarGridSpec(
            num_scalar_prefetch=1,
            grid=(exp_local,),
            in_specs=[
                pl.BlockSpec((1, 1, slots), lambda e, c: (e, 0, 0)),
                pl.BlockSpec((1, piece, slots), lambda e, c: (e, 0, 0)),
                pl.BlockSpec((1, task_count, piece, rank), lambda e, c: (e, 0, 0, 0)),
                pl.BlockSpec((1, task_count, rank, width), lambda e, c: (e, 0, 0, 0)),
                pl.BlockSpec((1, z_width, 1, piece, width), lambda e, c: (e, 0, c[0], 0, 0)),
                pl.BlockSpec((1, z_width, piece, width), lambda e, c: (e, 0, 0, 0)),
                pl.BlockSpec((1, slots, width), lambda e, c: (e, 0, 0)),
                pl.BlockSpec((1, slots, width), lambda e, c: (e, 0, 0)),
            ],
            out_specs=pl.BlockSpec((z_width, piece + more, slots), lambda e, c: (0, 0, e)),
        ),
        name="partial_sums",
    )(core.reshape(1), task_row, hidden, first, second, weight, weight_peer, rows, rows_peer)


def on_device(
    output_gradient,
    routed_expert_index,
    combine,
    token_task_index,
    saved_gate_input,
    saved_up_input,
    down_weight,
    adapter_first_factor,
    adapter_second_factor,
):
    exp_width = lax.axis_size("exp")
    z_width = lax.axis_size("z")
    core = lax.axis_index("core")
    exp_local, source_count, most, piece = saved_gate_input.shape
    tok_count, top = routed_expert_index.shape
    width = output_gradient.shape[1]
    task_count, rank = adapter_first_factor.shape[1], adapter_first_factor.shape[3]
    expert_count = exp_local * exp_width
    per_expert = source_count * most
    total_slots = exp_local * per_expert
    swap = [(0, 1), (1, 0)]

    weight = down_weight.reshape(exp_local, z_width, 2, piece, width)
    weight_peer = lax.ppermute(
        lax.dynamic_index_in_dim(weight, 1 - core, axis=2, keepdims=False), "core", swap
    )

    ids = routed_expert_index.T
    experts = jnp.arange(expert_count, dtype=jnp.int32)
    tokens = jnp.arange(tok_count, dtype=jnp.int32)
    names = ids[:, None, :] == experts[None, :, None]
    named = jnp.any(names, axis=0)
    gates = jnp.sum(jnp.where(names, combine.T[:, None, :].astype(F32), 0.0), axis=0)
    earlier = (tokens[:, None] < tokens[None, :]).astype(BF)
    place = jnp.dot(named.astype(BF), earlier, preferred_element_type=F32)
    place_or = jnp.where(named, place, -1.0).astype(BF)
    row_of = jnp.arange(expert_count * most, dtype=jnp.int32)
    spread = (row_of[:, None] // most == experts[None, :]).astype(BF)
    picked = jnp.dot(spread, place_or, preferred_element_type=F32) == (
        (row_of % most).astype(F32)[:, None]
    )
    send_rows = jnp.dot(picked.astype(BF), output_gradient, preferred_element_type=F32).astype(BF)
    slab = exp_local * most
    extra = -(exp_local + 1) % 8
    send = jnp.concatenate(
        [
            send_rows.reshape(exp_width, slab, width),
            gates.astype(BF).reshape(exp_width, exp_local, tok_count),
            jnp.broadcast_to(token_task_index.astype(BF), (exp_width, 1, tok_count)),
            jnp.zeros((exp_width, extra, tok_count), BF),
        ],
        axis=1,
    )
    received = lax.all_to_all(send, "exp", split_axis=0, concat_axis=0, tiled=True)

    rows = received[:, :slab].transpose(1, 0, 2).reshape(exp_local, per_expert, width)
    rows_peer = lax.ppermute(rows, "core", swap)
    gate_rows = received[:, slab : slab + exp_local].transpose(1, 0, 2)
    used = gate_rows > 0
    place_in = jnp.dot(
        used.astype(BF).reshape(exp_local * source_count, tok_count),
        earlier,
        preferred_element_type=F32,
    ).reshape(exp_local, source_count, tok_count)
    holds = used[:, None] & (
        place_in[:, None] == jnp.arange(most, dtype=jnp.int32).astype(F32)[:, None, None]
    )
    gate_slot = jnp.sum(jnp.where(holds, gate_rows.astype(F32)[:, None], 0.0), axis=3).reshape(
        exp_local, per_expert
    )
    task_rows = received[:, slab + exp_local].astype(F32)
    task_slot = jnp.sum(
        jnp.where(holds, task_rows, 0.0), axis=3
    ).reshape(exp_local, per_expert)
    task_mask = (
        task_slot[:, None] == jnp.arange(task_count, dtype=jnp.int32).astype(F32)[:, None]
    ).astype(F32)

    gate_f = saved_gate_input.transpose(0, 3, 2, 1).reshape(exp_local, piece, per_expert)
    up_f = saved_up_input.transpose(0, 3, 2, 1).reshape(exp_local, piece, per_expert)
    gate_f, up_f = gate_f.astype(F32), up_f.astype(F32)
    sig = jax.nn.sigmoid(gate_f)
    act = gate_f * sig
    hidden = (act * up_f).astype(BF)

    partial = partial_sums(
        core.astype(jnp.int32),
        task_slot[:, None],
        hidden,
        adapter_first_factor,
        adapter_second_factor,
        weight,
        weight_peer,
        rows,
        rows_peer,
    )
    summed = lax.psum_scatter(partial, "z", scatter_dimension=0, tiled=True)[0]
    back = summed[:piece].astype(F32).reshape(piece, exp_local, per_expert).transpose(1, 0, 2)

    pair_part = jnp.sum(hidden.astype(F32) * back, axis=1).reshape(1, total_slots)
    small = jnp.concatenate([summed[piece:], pair_part.astype(BF)])
    small = small.astype(F32) + lax.ppermute(small, "core", swap).astype(F32)
    everything = lax.all_gather(small.astype(BF), "z", axis=0, tiled=False)
    more = 2 * rank // z_width
    split = (rank, exp_local, per_expert)
    latent = everything[: z_width // 2, :more].reshape(split).astype(F32)
    query = everything[z_width // 2 :, :more].reshape(split).astype(F32)
    pair_sum = jnp.sum(everything[:, more].astype(F32), axis=0).reshape(exp_local, per_expert)
    weight_grad = pair_sum + jnp.sum(latent * query, axis=0)

    returned = lax.all_to_all(
        weight_grad.astype(BF).reshape(exp_local, most, source_count).transpose(2, 0, 1),
        "exp",
        split_axis=0,
        concat_axis=0,
        tiled=True,
    ).reshape(expert_count, most)

    scaled = (gate_slot * query).astype(BF)
    spread_update = (
        task_mask.transpose(1, 0, 2)[:, None] * scaled.astype(F32)[None]
    ).astype(BF)
    weighted = (gate_slot * latent).astype(BF)
    spread_z = (task_mask.transpose(1, 0, 2)[:, None] * weighted.astype(F32)[None]).astype(BF)
    first_grad = jnp.einsum(
        "tres,efs->etfr", spread_update, hidden, preferred_element_type=F32
    ).astype(BF)
    second_grad = jnp.einsum(
        "tres,esd->etrd", spread_z, rows, preferred_element_type=F32
    ).astype(BF)
    update_part = jnp.einsum(
        "tres,etfr->efs", spread_update, adapter_first_factor, preferred_element_type=F32
    )
    dh = gate_slot[:, None] * back + update_part
    gate_grad = (dh * up_f * sig * (1.0 + gate_f * (1.0 - sig))).astype(BF)
    up_grad = (dh * act).astype(BF)

    finder = names.transpose(1, 0, 2).reshape(expert_count, top * tok_count).astype(BF)
    place_pick = jnp.sum(jnp.where(names, place[None], 0.0), axis=1).reshape(1, top * tok_count)
    found = jnp.dot(returned.T, finder, preferred_element_type=F32)
    found = jnp.sum(
        jnp.where(jnp.arange(most, dtype=jnp.int32).astype(F32)[:, None] == place_pick, found, 0.0),
        axis=0,
    )
    grad_combine = found.reshape(top, tok_count).T
    shape_out = (exp_local, piece, most, source_count)
    return (
        gate_grad.reshape(shape_out).transpose(0, 3, 2, 1),
        up_grad.reshape(shape_out).transpose(0, 3, 2, 1),
        first_grad,
        second_grad,
        grad_combine,
    )


def solution(mesh):
    exp_width, seq_width = mesh.shape["exp"], mesh.shape["seq"]
    split = Mesh(mesh.devices.reshape(exp_width, seq_width // 2, 2), ("exp", "z", "core"))
    seq = ("z", "core")
    placed = (
        P("exp", seq),
        P("exp", None),
        P("exp", None),
        P("exp"),
        P("exp", None, None, seq),
        P("exp", None, None, seq),
        P("exp", None, seq),
        P("exp", None, seq, None),
        P("exp", None, None, seq),
    )
    return jax.shard_map(
        on_device,
        mesh=split,
        in_specs=placed,
        out_specs=(
            P("exp", None, None, seq),
            P("exp", None, None, seq),
            P("exp", None, seq, None),
            P("exp", None, None, seq),
            P("exp", None),
        ),
        check_vma=False,
    )
```

```python
import jax
import jax.numpy as jnp
from jax import lax
from jax.experimental import pallas as pl
from jax.experimental.pallas import tpu as pltpu
from jax.sharding import Mesh
from jax.sharding import PartitionSpec as P

BF = jnp.bfloat16
F32 = jnp.float32
PAD = 7


def partial_sums(core, task_row, hidden, first, second, weight, weight_peer, rows, rows_peer):
    exp_local, z_width, _, piece, width = weight.shape
    slots = rows.shape[1]
    task_count, rank = first.shape[1], first.shape[3]
    more = 2 * rank // z_width
    chunk = piece + more + PAD

    def kernel(core_ref, t_ref, h_ref, a_ref, b_ref, w_ref, wp_ref, x_ref, xp_ref, out_ref, f32_ref):
        nums = (((1,), (1,)), ((), ()))
        x = x_ref[0]
        own = w_ref[0, :, 0].reshape(z_width * piece, width)
        peer = wp_ref[0].reshape(z_width * piece, width)
        total = lax.dot_general(own, x, nums, preferred_element_type=F32)
        total += lax.dot_general(peer, xp_ref[0], nums, preferred_element_type=F32)
        ql_all = lax.dot_general(
            b_ref[0].reshape(task_count * rank, width), x, nums, preferred_element_type=F32
        )
        lat = jnp.zeros((rank, slots), F32)
        ql = jnp.zeros((rank, slots), F32)
        for t in range(task_count):
            keep = t_ref[0] == float(t)
            part = lax.dot_general(
                a_ref[0, t], h_ref[0], (((0,), (0,)), ((), ())), preferred_element_type=F32
            )
            lat += jnp.where(keep, part, 0.0)
            ql += jnp.where(keep, ql_all[t * rank : (t + 1) * rank], 0.0)
        small = jnp.concatenate([lat, ql])
        empty = jnp.zeros((PAD, slots), F32)
        for z in range(z_width):
            at = z * chunk
            f32_ref[at : at + piece] = total[z * piece : (z + 1) * piece]
            f32_ref[at + piece : at + piece + more] = small[z * more : (z + 1) * more]
            f32_ref[at + piece + more : at + chunk] = empty
        out_ref[...] = f32_ref[...].astype(BF)

    return pl.pallas_call(
        kernel,
        out_shape=jax.ShapeDtypeStruct((z_width * chunk, exp_local * slots), BF),
        grid_spec=pltpu.PrefetchScalarGridSpec(
            num_scalar_prefetch=1,
            grid=(exp_local,),
            in_specs=[
                pl.BlockSpec((1, 1, slots), lambda e, c: (e, 0, 0)),
                pl.BlockSpec((1, piece, slots), lambda e, c: (e, 0, 0)),
                pl.BlockSpec((1, task_count, piece, rank), lambda e, c: (e, 0, 0, 0)),
                pl.BlockSpec((1, task_count, rank, width), lambda e, c: (e, 0, 0, 0)),
                pl.BlockSpec((1, z_width, 1, piece, width), lambda e, c: (e, 0, c[0], 0, 0)),
                pl.BlockSpec((1, z_width, piece, width), lambda e, c: (e, 0, 0, 0)),
                pl.BlockSpec((1, slots, width), lambda e, c: (e, 0, 0)),
                pl.BlockSpec((1, slots, width), lambda e, c: (e, 0, 0)),
            ],
            out_specs=pl.BlockSpec((z_width * chunk, slots), lambda e, c: (0, e)),
            scratch_shapes=[pltpu.VMEM((z_width * chunk, slots), F32)],
        ),
        name="partial_sums",
    )(core.reshape(1), task_row, hidden, first, second, weight, weight_peer, rows, rows_peer)


def on_device(
    output_gradient,
    routed_expert_index,
    combine,
    token_task_index,
    saved_gate_input,
    saved_up_input,
    down_weight,
    adapter_first_factor,
    adapter_second_factor,
):
    exp_width = lax.axis_size("exp")
    z_width = lax.axis_size("z")
    core = lax.axis_index("core")
    exp_local, source_count, most, piece = saved_gate_input.shape
    tok_count, top = routed_expert_index.shape
    width = output_gradient.shape[1]
    task_count, rank = adapter_first_factor.shape[1], adapter_first_factor.shape[3]
    expert_count = exp_local * exp_width
    per_expert = source_count * most
    total_slots = exp_local * per_expert
    swap = [(0, 1), (1, 0)]

    weight = down_weight.reshape(exp_local, z_width, 2, piece, width)
    weight_peer = lax.ppermute(
        lax.dynamic_index_in_dim(weight, 1 - core, axis=2, keepdims=False), "core", swap
    )

    ids = routed_expert_index.T
    experts = jnp.arange(expert_count, dtype=jnp.int32)
    tokens = jnp.arange(tok_count, dtype=jnp.int32)
    names = ids[:, None, :] == experts[None, :, None]
    named = jnp.any(names, axis=0)
    gates = jnp.sum(jnp.where(names, combine.T[:, None, :].astype(F32), 0.0), axis=0)
    earlier = (tokens[:, None] < tokens[None, :]).astype(BF)
    place = jnp.dot(named.astype(BF), earlier, preferred_element_type=F32)
    place_or = jnp.where(named, place, -1.0).astype(BF)
    row_of = jnp.arange(expert_count * most, dtype=jnp.int32)
    spread = (row_of[:, None] // most == experts[None, :]).astype(BF)
    picked = jnp.dot(spread, place_or, preferred_element_type=F32) == (
        (row_of % most).astype(F32)[:, None]
    )
    send_rows = jnp.dot(picked.astype(BF), output_gradient, preferred_element_type=F32).astype(BF)
    slab = exp_local * most
    extra = -(exp_local + 1) % 8
    send = jnp.concatenate(
        [
            send_rows.reshape(exp_width, slab, width),
            gates.astype(BF).reshape(exp_width, exp_local, tok_count),
            jnp.broadcast_to(token_task_index.astype(BF), (exp_width, 1, tok_count)),
            jnp.zeros((exp_width, extra, tok_count), BF),
        ],
        axis=1,
    )
    received = lax.all_to_all(send, "exp", split_axis=0, concat_axis=0, tiled=True)

    rows = received[:, :slab].transpose(1, 0, 2).reshape(exp_local, per_expert, width)
    rows_peer = lax.ppermute(rows, "core", swap)
    gate_rows = received[:, slab : slab + exp_local].transpose(1, 0, 2)
    used = gate_rows > 0
    place_in = jnp.dot(
        used.astype(BF).reshape(exp_local * source_count, tok_count),
        earlier,
        preferred_element_type=F32,
    ).reshape(exp_local, source_count, tok_count)
    holds = used[:, None] & (
        place_in[:, None] == jnp.arange(most, dtype=jnp.int32).astype(F32)[:, None, None]
    )
    gate_slot = jnp.sum(jnp.where(holds, gate_rows.astype(F32)[:, None], 0.0), axis=3).reshape(
        exp_local, per_expert
    )
    task_rows = received[:, slab + exp_local].astype(F32)
    task_slot = jnp.sum(
        jnp.where(holds, task_rows, 0.0), axis=3
    ).reshape(exp_local, per_expert)
    task_mask = (
        task_slot[:, None] == jnp.arange(task_count, dtype=jnp.int32).astype(F32)[:, None]
    ).astype(F32)

    gate_f = saved_gate_input.transpose(0, 3, 2, 1).reshape(exp_local, piece, per_expert)
    up_f = saved_up_input.transpose(0, 3, 2, 1).reshape(exp_local, piece, per_expert)
    gate_f, up_f = gate_f.astype(F32), up_f.astype(F32)
    sig = jax.nn.sigmoid(gate_f)
    act = gate_f * sig
    hidden = (act * up_f).astype(BF)

    partial = partial_sums(
        core.astype(jnp.int32),
        task_slot[:, None],
        hidden,
        adapter_first_factor,
        adapter_second_factor,
        weight,
        weight_peer,
        rows,
        rows_peer,
    )
    summed = lax.psum_scatter(partial, "z", scatter_dimension=0, tiled=True)
    summed = lax.optimization_barrier(summed)
    back = summed[:piece].astype(F32).reshape(piece, exp_local, per_expert).transpose(1, 0, 2)

    pair_part = jnp.sum(hidden.astype(F32) * back, axis=1).reshape(1, total_slots)
    more = 2 * rank // z_width
    small = jnp.concatenate([summed[piece : piece + more], pair_part.astype(BF)])
    small = small.reshape(-1, 128)
    small = small.astype(F32) + lax.ppermute(small, "core", swap).astype(F32)
    everything = lax.all_gather(small.astype(BF), "z", axis=0, tiled=False)
    everything = everything.reshape(z_width, more + 1, total_slots)
    split = (rank, exp_local, per_expert)
    latent = everything[: z_width // 2, :more].reshape(split).astype(F32)
    query = everything[z_width // 2 :, :more].reshape(split).astype(F32)
    pair_sum = jnp.sum(everything[:, more].astype(F32), axis=0).reshape(exp_local, per_expert)
    weight_grad = pair_sum + jnp.sum(latent * query, axis=0)

    returned = lax.all_to_all(
        weight_grad.astype(BF).reshape(exp_local, most, source_count).transpose(2, 0, 1),
        "exp",
        split_axis=0,
        concat_axis=0,
        tiled=True,
    ).reshape(expert_count, most)

    scaled = (gate_slot * query).astype(BF)
    spread_update = (
        task_mask.transpose(1, 0, 2)[:, None] * scaled.astype(F32)[None]
    ).astype(BF)
    weighted = (gate_slot * latent).astype(BF)
    spread_z = (task_mask.transpose(1, 0, 2)[:, None] * weighted.astype(F32)[None]).astype(BF)
    first_grad = jnp.einsum(
        "tres,efs->etfr", spread_update, hidden, preferred_element_type=F32
    ).astype(BF)
    second_grad = jnp.einsum(
        "tres,esd->etrd", spread_z, rows, preferred_element_type=F32
    ).astype(BF)
    update_part = jnp.einsum(
        "tres,etfr->efs", spread_update, adapter_first_factor, preferred_element_type=F32
    )
    dh = gate_slot[:, None] * back + update_part
    gate_grad = (dh * up_f * sig * (1.0 + gate_f * (1.0 - sig))).astype(BF)
    up_grad = (dh * act).astype(BF)

    finder = names.transpose(1, 0, 2).reshape(expert_count, top * tok_count).astype(BF)
    place_pick = jnp.sum(jnp.where(names, place[None], 0.0), axis=1).reshape(1, top * tok_count)
    found = jnp.dot(returned.T, finder, preferred_element_type=F32)
    found = jnp.sum(
        jnp.where(jnp.arange(most, dtype=jnp.int32).astype(F32)[:, None] == place_pick, found, 0.0),
        axis=0,
    )
    grad_combine = found.reshape(top, tok_count).T
    shape_out = (exp_local, piece, most, source_count)
    return (
        gate_grad.reshape(shape_out).transpose(0, 3, 2, 1),
        up_grad.reshape(shape_out).transpose(0, 3, 2, 1),
        first_grad,
        second_grad,
        grad_combine,
    )


def solution(mesh):
    exp_width, seq_width = mesh.shape["exp"], mesh.shape["seq"]
    split = Mesh(mesh.devices.reshape(exp_width, seq_width // 2, 2), ("exp", "z", "core"))
    seq = ("z", "core")
    placed = (
        P("exp", seq),
        P("exp", None),
        P("exp", None),
        P("exp"),
        P("exp", None, None, seq),
        P("exp", None, None, seq),
        P("exp", None, seq),
        P("exp", None, seq, None),
        P("exp", None, None, seq),
    )
    return jax.shard_map(
        on_device,
        mesh=split,
        in_specs=placed,
        out_specs=(
            P("exp", None, None, seq),
            P("exp", None, None, seq),
            P("exp", None, seq, None),
            P("exp", None, None, seq),
            P("exp", None),
        ),
        check_vma=False,
    )
```

```python
import jax
import jax.numpy as jnp
from jax import lax
from jax.experimental import pallas as pl
from jax.experimental.pallas import tpu as pltpu
from jax.sharding import Mesh
from jax.sharding import PartitionSpec as P

BF = jnp.bfloat16
F32 = jnp.float32
PAD = 7


def partial_sums(core, task_row, hidden, first, second, weight, weight_peer, rows, rows_peer, order):
    exp_local, z_width, _, piece, width = weight.shape
    slots = rows.shape[1]
    task_count, rank = first.shape[1], first.shape[3]
    more = 2 * rank // z_width
    chunk = piece + more + PAD

    def kernel(core_ref, t_ref, h_ref, a_ref, b_ref, w_ref, wp_ref, x_ref, xp_ref, out_ref, f32_ref):
        nums = (((1,), (1,)), ((), ()))
        core_at = core_ref[0]
        for z in range(z_width):
            f32_ref[(z + 1) * chunk - PAD : (z + 1) * chunk] = jnp.zeros((PAD, slots), F32)
        for e in range(exp_local):
            x = x_ref[e]
            own = w_ref[e, :, core_at].reshape(z_width * piece, width)
            peer = wp_ref[e].reshape(z_width * piece, width)
            total = lax.dot_general(own, x, nums, preferred_element_type=F32)
            total += lax.dot_general(peer, xp_ref[e], nums, preferred_element_type=F32)
            ql_all = lax.dot_general(
                b_ref[e].reshape(task_count * rank, width), x, nums, preferred_element_type=F32
            )
            lat = jnp.zeros((rank, slots), F32)
            ql = jnp.zeros((rank, slots), F32)
            for t in range(task_count):
                keep = t_ref[e : e + 1] == float(t)
                part = lax.dot_general(
                    a_ref[e, t], h_ref[e], (((0,), (0,)), ((), ())), preferred_element_type=F32
                )
                lat += jnp.where(keep, part, 0.0)
                ql += jnp.where(keep, ql_all[t * rank : (t + 1) * rank], 0.0)
            small = jnp.concatenate([lat, ql])
            for z in range(z_width):
                at, line = z * chunk, order[z] * more
                f32_ref[at : at + piece] = total[z * piece : (z + 1) * piece]
                f32_ref[at + piece : at + piece + more] = small[line : line + more]
            out_ref[:, e * slots : (e + 1) * slots] = f32_ref[...].astype(BF)

    vmem = pl.BlockSpec(memory_space=pltpu.VMEM)
    return pl.pallas_call(
        kernel,
        out_shape=jax.ShapeDtypeStruct((z_width * chunk, exp_local * slots), BF),
        in_specs=[pl.BlockSpec(memory_space=pltpu.SMEM)] + [vmem] * 8,
        out_specs=vmem,
        scratch_shapes=[pltpu.VMEM((z_width * chunk, slots), F32)],
        name="partial_sums",
    )(core.reshape(1), task_row, hidden, first, second, weight, weight_peer, rows, rows_peer)


def on_device(
    output_gradient,
    routed_expert_index,
    combine,
    token_task_index,
    saved_gate_input,
    saved_up_input,
    down_weight,
    adapter_first_factor,
    adapter_second_factor,
):
    exp_width = lax.axis_size("exp")
    zh_width, zl_width = lax.axis_size("zh"), lax.axis_size("zl")
    z_width = zh_width * zl_width
    core = lax.axis_index("core")
    exp_local, source_count, most, piece = saved_gate_input.shape
    tok_count, top = routed_expert_index.shape
    width = output_gradient.shape[1]
    task_count, rank = adapter_first_factor.shape[1], adapter_first_factor.shape[3]
    expert_count = exp_local * exp_width
    per_expert = source_count * most
    total_slots = exp_local * per_expert
    swap = [(0, 1), (1, 0)]

    weight = down_weight.reshape(exp_local, z_width, 2, piece, width)
    weight_peer = lax.ppermute(
        lax.dynamic_index_in_dim(weight, 1 - core, axis=2, keepdims=False), "core", swap
    )

    ids = routed_expert_index.T
    experts = jnp.arange(expert_count, dtype=jnp.int32)
    tokens = jnp.arange(tok_count, dtype=jnp.int32)
    names = ids[:, None, :] == experts[None, :, None]
    named = jnp.any(names, axis=0)
    gates = jnp.sum(jnp.where(names, combine.T[:, None, :].astype(F32), 0.0), axis=0)
    earlier = (tokens[:, None] < tokens[None, :]).astype(BF)
    place = jnp.dot(named.astype(BF), earlier, preferred_element_type=F32)
    place_or = jnp.where(named, place, -1.0).astype(BF)
    row_of = jnp.arange(expert_count * most, dtype=jnp.int32)
    spread = (row_of[:, None] // most == experts[None, :]).astype(BF)
    picked = jnp.dot(spread, place_or, preferred_element_type=F32) == (
        (row_of % most).astype(F32)[:, None]
    )
    send_rows = jnp.dot(picked.astype(BF), output_gradient, preferred_element_type=F32).astype(BF)
    slab = exp_local * most
    extra = -(exp_local + 1) % 8
    send = jnp.concatenate(
        [
            send_rows.reshape(exp_width, slab, width),
            gates.astype(BF).reshape(exp_width, exp_local, tok_count),
            jnp.broadcast_to(token_task_index.astype(BF), (exp_width, 1, tok_count)),
            jnp.zeros((exp_width, extra, tok_count), BF),
        ],
        axis=1,
    )
    received = lax.all_to_all(send, "exp", split_axis=0, concat_axis=0, tiled=True)

    rows = received[:, :slab].transpose(1, 0, 2).reshape(exp_local, per_expert, width)
    rows_peer = lax.ppermute(rows, "core", swap)
    gate_rows = received[:, slab : slab + exp_local].transpose(1, 0, 2)
    used = gate_rows > 0
    place_in = jnp.dot(
        used.astype(BF).reshape(exp_local * source_count, tok_count),
        earlier,
        preferred_element_type=F32,
    ).reshape(exp_local, source_count, tok_count)
    holds = used[:, None] & (
        place_in[:, None] == jnp.arange(most, dtype=jnp.int32).astype(F32)[:, None, None]
    )
    gate_slot = jnp.sum(jnp.where(holds, gate_rows.astype(F32)[:, None], 0.0), axis=3).reshape(
        exp_local, per_expert
    )
    task_rows = received[:, slab + exp_local].astype(F32)
    task_slot = jnp.sum(
        jnp.where(holds, task_rows, 0.0), axis=3
    ).reshape(exp_local, per_expert)
    task_mask = (
        task_slot[:, None] == jnp.arange(task_count, dtype=jnp.int32).astype(F32)[:, None]
    ).astype(F32)

    gate_f = saved_gate_input.transpose(0, 3, 2, 1).reshape(exp_local, piece, per_expert)
    up_f = saved_up_input.transpose(0, 3, 2, 1).reshape(exp_local, piece, per_expert)
    gate_f, up_f = gate_f.astype(F32), up_f.astype(F32)
    sig = jax.nn.sigmoid(gate_f)
    act = gate_f * sig
    hidden = (act * up_f).astype(BF)

    partial = partial_sums(
        core.astype(jnp.int32),
        task_slot,
        hidden,
        adapter_first_factor,
        adapter_second_factor,
        weight,
        weight_peer,
        rows,
        rows_peer,
        [z % zl_width * zh_width + z // zl_width for z in range(z_width)],
    )
    summed = lax.psum_scatter(partial, ("zh", "zl"), scatter_dimension=0, tiled=True)
    summed = lax.optimization_barrier(summed)
    back = summed[:piece].astype(F32).reshape(piece, exp_local, per_expert).transpose(1, 0, 2)

    pair_part = jnp.sum(hidden.astype(F32) * back, axis=1).reshape(1, total_slots)
    more = 2 * rank // z_width
    small = jnp.concatenate([summed[piece : piece + more], pair_part.astype(BF)])
    small = small.reshape(-1, 128)
    small = small.astype(F32) + lax.ppermute(small, "core", swap).astype(F32)
    everything = lax.all_gather(small.astype(BF), "zh", axis=0, tiled=False)
    everything = lax.all_gather(everything, "zl", axis=0, tiled=False)
    everything = everything.reshape(z_width, more + 1, total_slots)
    split = (rank, exp_local, per_expert)
    latent = everything[: z_width // 2, :more].reshape(split).astype(F32)
    query = everything[z_width // 2 :, :more].reshape(split).astype(F32)
    pair_sum = jnp.sum(everything[:, more].astype(F32), axis=0).reshape(exp_local, per_expert)
    weight_grad = pair_sum + jnp.sum(latent * query, axis=0)

    returned = lax.all_to_all(
        weight_grad.astype(BF).reshape(exp_local, most, source_count).transpose(2, 0, 1),
        "exp",
        split_axis=0,
        concat_axis=0,
        tiled=True,
    ).reshape(expert_count, most)

    scaled = (gate_slot * query).astype(BF)
    spread_update = (
        task_mask.transpose(1, 0, 2)[:, None] * scaled.astype(F32)[None]
    ).astype(BF)
    weighted = (gate_slot * latent).astype(BF)
    spread_z = (task_mask.transpose(1, 0, 2)[:, None] * weighted.astype(F32)[None]).astype(BF)
    first_grad = jnp.einsum(
        "tres,efs->etfr", spread_update, hidden, preferred_element_type=F32
    ).astype(BF)
    second_grad = jnp.einsum(
        "tres,esd->etrd", spread_z, rows, preferred_element_type=F32
    ).astype(BF)
    update_part = jnp.einsum(
        "tres,etfr->efs", spread_update, adapter_first_factor, preferred_element_type=F32
    )
    dh = gate_slot[:, None] * back + update_part
    gate_grad = (dh * up_f * sig * (1.0 + gate_f * (1.0 - sig))).astype(BF)
    up_grad = (dh * act).astype(BF)

    finder = names.transpose(1, 0, 2).reshape(expert_count, top * tok_count).astype(BF)
    place_pick = jnp.sum(jnp.where(names, place[None], 0.0), axis=1).reshape(1, top * tok_count)
    found = jnp.dot(returned.T, finder, preferred_element_type=F32)
    found = jnp.sum(
        jnp.where(jnp.arange(most, dtype=jnp.int32).astype(F32)[:, None] == place_pick, found, 0.0),
        axis=0,
    )
    grad_combine = found.reshape(top, tok_count).T
    shape_out = (exp_local, piece, most, source_count)
    return (
        gate_grad.reshape(shape_out).transpose(0, 3, 2, 1),
        up_grad.reshape(shape_out).transpose(0, 3, 2, 1),
        first_grad,
        second_grad,
        grad_combine,
    )


def solution(mesh):
    exp_width, seq_width = mesh.shape["exp"], mesh.shape["seq"]
    split = Mesh(
        mesh.devices.reshape(exp_width, 4, seq_width // 8, 2), ("exp", "zh", "zl", "core")
    )
    seq = ("zh", "zl", "core")
    placed = (
        P("exp", seq),
        P("exp", None),
        P("exp", None),
        P("exp"),
        P("exp", None, None, seq),
        P("exp", None, None, seq),
        P("exp", None, seq),
        P("exp", None, seq, None),
        P("exp", None, None, seq),
    )
    return jax.shard_map(
        on_device,
        mesh=split,
        in_specs=placed,
        out_specs=(
            P("exp", None, None, seq),
            P("exp", None, None, seq),
            P("exp", None, seq, None),
            P("exp", None, None, seq),
            P("exp", None),
        ),
        check_vma=False,
    )
```

```python
import jax
import jax.numpy as jnp
from jax import lax
from jax.experimental import pallas as pl
from jax.experimental.pallas import tpu as pltpu
from jax.sharding import Mesh
from jax.sharding import PartitionSpec as P

BF = jnp.bfloat16
F32 = jnp.float32
PAD = 7


def partial_sums(core, task_row, hidden, first, second, weight, weight_peer, rows, rows_peer):
    exp_local, z_width, _, piece, width = weight.shape
    slots = rows.shape[1]
    task_count, rank = first.shape[1], first.shape[2]
    more = 2 * rank // z_width
    chunk = piece + more + PAD

    def kernel(core_ref, t_ref, h_ref, a_ref, b_ref, w_ref, wp_ref, x_ref, xp_ref, out_ref, f32_ref):
        nums = (((1,), (1,)), ((), ()))
        x = x_ref[0]
        own = w_ref[0, :, 0].reshape(z_width * piece, width)
        peer = wp_ref[0].reshape(z_width * piece, width)
        total = lax.dot_general(
            jnp.concatenate([own, peer], axis=1),
            jnp.concatenate([x, xp_ref[0]], axis=1),
            nums,
            preferred_element_type=F32,
        )
        ql_all = lax.dot_general(
            b_ref[0].reshape(task_count * rank, width), x, nums, preferred_element_type=F32
        )
        lat_all = jnp.dot(
            a_ref[0].reshape(task_count * rank, piece), h_ref[0], preferred_element_type=F32
        )
        lat = jnp.zeros((rank, slots), F32)
        ql = jnp.zeros((rank, slots), F32)
        for t in range(task_count):
            keep = t_ref[0] == float(t)
            lat += jnp.where(keep, lat_all[t * rank : (t + 1) * rank], 0.0)
            ql += jnp.where(keep, ql_all[t * rank : (t + 1) * rank], 0.0)
        small = jnp.concatenate([lat, ql])
        empty = jnp.zeros((PAD, slots), F32)
        for z in range(z_width):
            at = z * chunk
            f32_ref[at : at + piece] = total[z * piece : (z + 1) * piece]
            f32_ref[at + piece : at + piece + more] = small[z * more : (z + 1) * more]
            f32_ref[at + piece + more : at + chunk] = empty
        out_ref[...] = f32_ref[...].astype(BF)

    return pl.pallas_call(
        kernel,
        out_shape=jax.ShapeDtypeStruct((z_width * chunk, exp_local * slots), BF),
        grid_spec=pltpu.PrefetchScalarGridSpec(
            num_scalar_prefetch=1,
            grid=(exp_local,),
            in_specs=[
                pl.BlockSpec((1, 1, slots), lambda e, c: (e, 0, 0)),
                pl.BlockSpec((1, piece, slots), lambda e, c: (e, 0, 0)),
                pl.BlockSpec((1, task_count, rank, piece), lambda e, c: (e, 0, 0, 0)),
                pl.BlockSpec((1, task_count, rank, width), lambda e, c: (e, 0, 0, 0)),
                pl.BlockSpec((1, z_width, 1, piece, width), lambda e, c: (e, 0, c[0], 0, 0)),
                pl.BlockSpec((1, z_width, piece, width), lambda e, c: (e, 0, 0, 0)),
                pl.BlockSpec((1, slots, width), lambda e, c: (e, 0, 0)),
                pl.BlockSpec((1, slots, width), lambda e, c: (e, 0, 0)),
            ],
            out_specs=pl.BlockSpec((z_width * chunk, slots), lambda e, c: (0, e)),
            scratch_shapes=[pltpu.VMEM((z_width * chunk, slots), F32)],
        ),
        name="partial_sums",
    )(core.reshape(1), task_row, hidden, first, second, weight, weight_peer, rows, rows_peer)


def dispatch_slab(ids, gates, tasks, gradient, expert_count, exp_width, most):
    top, tok_count = ids.shape
    width = gradient.shape[1]
    local = expert_count // exp_width
    slab = local * most
    lines = slab + local + 1
    lines += -lines % 8

    def kernel(id_ref, gate_ref, task_ref, grad_ref, out_ref):
        expert = lax.broadcasted_iota(jnp.int32, (expert_count, tok_count), 0)
        gate = gate_ref[...].astype(F32)
        named = jnp.zeros((expert_count, tok_count), F32)
        weight = jnp.zeros((expert_count, tok_count), F32)
        for k in range(top):
            here = id_ref[k : k + 1] == expert
            named += jnp.where(here, 1.0, 0.0)
            weight += jnp.where(here, gate[k : k + 1], 0.0)
        before = lax.broadcasted_iota(jnp.int32, (tok_count, tok_count), 0)
        after = lax.broadcasted_iota(jnp.int32, (tok_count, tok_count), 1)
        earlier = jnp.where(before < after, 1.0, 0.0).astype(BF)
        place = jnp.dot(named.astype(BF), earlier, preferred_element_type=F32)
        place = jnp.where(named > 0.0, place, -1.0).astype(BF)
        row = lax.broadcasted_iota(jnp.int32, (expert_count * most, expert_count), 0)
        col = lax.broadcasted_iota(jnp.int32, (expert_count * most, expert_count), 1)
        offset = row - col * most
        spread = jnp.where((offset >= 0) & (offset < most), 1.0, 0.0).astype(BF)
        column = lax.broadcasted_iota(jnp.int32, (expert_count, 128), 0)
        place_row = jnp.dot(spread, place, preferred_element_type=F32)
        first = jnp.dot(spread, column.astype(F32).astype(BF), preferred_element_type=F32)
        row_at = lax.broadcasted_iota(jnp.int32, (expert_count * most, tok_count), 0).astype(F32)
        picked = jnp.where(place_row == row_at - first * float(most), 1.0, 0.0).astype(BF)
        rows = jnp.dot(picked, grad_ref[...], preferred_element_type=F32).astype(BF)
        out_ref[:, :slab] = rows.reshape(exp_width, slab, width)
        task = task_ref[...].astype(F32)
        empty = jnp.zeros((lines - slab - local - 1, tok_count), F32)
        for g in range(exp_width):
            tail = [weight[g * local : (g + 1) * local], task, empty]
            out_ref[g, slab:] = jnp.concatenate(tail).astype(BF)

    return pl.pallas_call(
        kernel,
        out_shape=jax.ShapeDtypeStruct((exp_width, lines, width), BF),
        name="dispatch_slab",
    )(ids, gates, tasks, gradient)


def on_device(
    output_gradient,
    routed_expert_index,
    combine,
    token_task_index,
    saved_gate_input,
    saved_up_input,
    down_weight,
    adapter_first_factor,
    adapter_second_factor,
):
    exp_width = lax.axis_size("exp")
    z_width = lax.axis_size("z")
    core = lax.axis_index("core")
    exp_local, source_count, most, piece = saved_gate_input.shape
    tok_count, top = routed_expert_index.shape
    width = output_gradient.shape[1]
    task_count, rank = adapter_first_factor.shape[1], adapter_first_factor.shape[3]
    expert_count = exp_local * exp_width
    per_expert = source_count * most
    total_slots = exp_local * per_expert
    swap = [(0, 1), (1, 0)]

    weight = down_weight.reshape(exp_local, z_width, 2, piece, width)
    weight_peer = lax.ppermute(
        lax.dynamic_index_in_dim(weight, 1 - core, axis=2, keepdims=False), "core", swap
    )

    ids = routed_expert_index.T
    experts = jnp.arange(expert_count, dtype=jnp.int32)
    tokens = jnp.arange(tok_count, dtype=jnp.int32)
    names = ids[:, None, :] == experts[None, :, None]
    named = jnp.any(names, axis=0)
    earlier = (tokens[:, None] < tokens[None, :]).astype(BF)
    place = jnp.dot(named.astype(BF), earlier, preferred_element_type=F32)
    slab = exp_local * most
    send = dispatch_slab(
        ids,
        combine.T,
        token_task_index[None],
        output_gradient,
        expert_count,
        exp_width,
        most,
    )
    received = lax.all_to_all(send, "exp", split_axis=0, concat_axis=0, tiled=True)

    rows = received[:, :slab].transpose(1, 0, 2).reshape(exp_local, per_expert, width)
    rows_peer = lax.ppermute(rows, "core", swap)
    gate_rows = received[:, slab : slab + exp_local].transpose(1, 0, 2)
    used = gate_rows > 0
    place_in = jnp.dot(
        used.astype(BF).reshape(exp_local * source_count, tok_count),
        earlier,
        preferred_element_type=F32,
    ).reshape(exp_local, source_count, tok_count)
    holds = used[:, None] & (
        place_in[:, None] == jnp.arange(most, dtype=jnp.int32).astype(F32)[:, None, None]
    )
    gate_slot = jnp.sum(jnp.where(holds, gate_rows.astype(F32)[:, None], 0.0), axis=3).reshape(
        exp_local, per_expert
    )
    task_rows = received[:, slab + exp_local].astype(F32)
    task_slot = jnp.sum(
        jnp.where(holds, task_rows, 0.0), axis=3
    ).reshape(exp_local, per_expert)
    task_mask = (
        task_slot[:, None] == jnp.arange(task_count, dtype=jnp.int32).astype(F32)[:, None]
    ).astype(F32)

    gate_f = saved_gate_input.transpose(0, 3, 2, 1).reshape(exp_local, piece, per_expert)
    up_f = saved_up_input.transpose(0, 3, 2, 1).reshape(exp_local, piece, per_expert)
    gate_f, up_f = gate_f.astype(F32), up_f.astype(F32)
    sig = jax.nn.sigmoid(gate_f)
    act = gate_f * sig
    hidden = (act * up_f).astype(BF)

    partial = partial_sums(
        core.astype(jnp.int32),
        task_slot[:, None],
        hidden,
        adapter_first_factor.swapaxes(2, 3),
        adapter_second_factor,
        weight,
        weight_peer,
        rows,
        rows_peer,
    )
    summed = lax.psum_scatter(partial, "z", scatter_dimension=0, tiled=True)
    summed = lax.optimization_barrier(summed)
    back = summed[:piece].astype(F32).reshape(piece, exp_local, per_expert).transpose(1, 0, 2)

    pair_part = jnp.sum(hidden.astype(F32) * back, axis=1).reshape(1, total_slots)
    more = 2 * rank // z_width
    small = jnp.concatenate([summed[piece : piece + more], pair_part.astype(BF)])
    small = small.reshape(2, -1, 128)
    theirs = lax.dynamic_index_in_dim(small, 1 - core, axis=0, keepdims=False)
    mine = lax.dynamic_index_in_dim(small, core, axis=0, keepdims=False).astype(F32)
    mine = (mine + lax.ppermute(theirs, "core", swap).astype(F32)).astype(BF)
    half = lax.all_gather(mine, "z", axis=0, tiled=False)
    other = lax.ppermute(half, "core", swap)
    everything = jnp.where(
        core == 0, jnp.stack([half, other], axis=1), jnp.stack([other, half], axis=1)
    )
    everything = everything.reshape(z_width, more + 1, total_slots)
    split = (rank, exp_local, per_expert)
    latent = everything[: z_width // 2, :more].reshape(split).astype(F32)
    query = everything[z_width // 2 :, :more].reshape(split).astype(F32)
    pair_sum = jnp.sum(everything[:, more].astype(F32), axis=0).reshape(exp_local, per_expert)
    weight_grad = pair_sum + jnp.sum(latent * query, axis=0)

    returned = lax.all_to_all(
        weight_grad.astype(BF).reshape(exp_local, most, source_count).transpose(2, 0, 1),
        "exp",
        split_axis=0,
        concat_axis=0,
        tiled=True,
    ).reshape(expert_count, most)

    scaled = (gate_slot * query).astype(BF)
    spread_update = (
        task_mask.transpose(1, 0, 2)[:, None] * scaled.astype(F32)[None]
    ).astype(BF)
    weighted = (gate_slot * latent).astype(BF)
    spread_z = (task_mask.transpose(1, 0, 2)[:, None] * weighted.astype(F32)[None]).astype(BF)
    first_grad = jnp.einsum(
        "tres,efs->etfr", spread_update, hidden, preferred_element_type=F32
    ).astype(BF)
    second_grad = jnp.einsum(
        "tres,esd->etrd", spread_z, rows, preferred_element_type=F32
    ).astype(BF)
    update_part = jnp.einsum(
        "tres,etfr->efs", spread_update, adapter_first_factor, preferred_element_type=F32
    )
    dh = gate_slot[:, None] * back + update_part
    gate_grad = (dh * up_f * sig * (1.0 + gate_f * (1.0 - sig))).astype(BF)
    up_grad = (dh * act).astype(BF)

    finder = names.transpose(1, 0, 2).reshape(expert_count, top * tok_count).astype(BF)
    place_pick = jnp.sum(jnp.where(names, place[None], 0.0), axis=1).reshape(1, top * tok_count)
    found = jnp.dot(returned.T, finder, preferred_element_type=F32)
    found = jnp.sum(
        jnp.where(jnp.arange(most, dtype=jnp.int32).astype(F32)[:, None] == place_pick, found, 0.0),
        axis=0,
    )
    grad_combine = found.reshape(top, tok_count).T
    shape_out = (exp_local, piece, most, source_count)
    return (
        gate_grad.reshape(shape_out).transpose(0, 3, 2, 1),
        up_grad.reshape(shape_out).transpose(0, 3, 2, 1),
        first_grad,
        second_grad,
        grad_combine,
    )


def solution(mesh):
    exp_width, seq_width = mesh.shape["exp"], mesh.shape["seq"]
    split = Mesh(mesh.devices.reshape(exp_width, seq_width // 2, 2), ("exp", "z", "core"))
    seq = ("z", "core")
    placed = (
        P("exp", seq),
        P("exp", None),
        P("exp", None),
        P("exp"),
        P("exp", None, None, seq),
        P("exp", None, None, seq),
        P("exp", None, seq),
        P("exp", None, seq, None),
        P("exp", None, None, seq),
    )
    return jax.shard_map(
        on_device,
        mesh=split,
        in_specs=placed,
        out_specs=(
            P("exp", None, None, seq),
            P("exp", None, None, seq),
            P("exp", None, seq, None),
            P("exp", None, None, seq),
            P("exp", None),
        ),
        check_vma=False,
    )
```

```python
import jax
import jax.numpy as jnp
from jax import lax
from jax.experimental import pallas as pl
from jax.experimental.pallas import tpu as pltpu
from jax.sharding import Mesh
from jax.sharding import PartitionSpec as P

BF = jnp.bfloat16
F32 = jnp.float32
PAD = 7


def partial_sums(core, task_row, hidden, first, second, weight, weight_peer, rows, rows_peer):
    exp_local, z_width, _, piece, width = weight.shape
    slots = rows.shape[1]
    task_count, rank = first.shape[1], first.shape[2]
    more = 2 * rank // z_width
    chunk = piece + more + PAD

    def kernel(core_ref, t_ref, h_ref, a_ref, b_ref, w_ref, wp_ref, x_ref, xp_ref, out_ref, f32_ref):
        nums = (((1,), (1,)), ((), ()))
        x = x_ref[0]
        own = w_ref[0, :, 0].reshape(z_width * piece, width)
        peer = wp_ref[0].reshape(z_width * piece, width)
        total = lax.dot_general(
            jnp.concatenate([own, peer], axis=1),
            jnp.concatenate([x, xp_ref[0]], axis=1),
            nums,
            preferred_element_type=F32,
        )
        ql_all = lax.dot_general(
            b_ref[0].reshape(task_count * rank, width), x, nums, preferred_element_type=F32
        )
        lat_all = jnp.dot(
            a_ref[0].reshape(task_count * rank, piece), h_ref[0], preferred_element_type=F32
        )
        lat = jnp.zeros((rank, slots), F32)
        ql = jnp.zeros((rank, slots), F32)
        for t in range(task_count):
            keep = t_ref[0] == float(t)
            lat += jnp.where(keep, lat_all[t * rank : (t + 1) * rank], 0.0)
            ql += jnp.where(keep, ql_all[t * rank : (t + 1) * rank], 0.0)
        small = jnp.concatenate([lat, ql])
        empty = jnp.zeros((PAD, slots), F32)
        for z in range(z_width):
            at = z * chunk
            f32_ref[at : at + piece] = total[z * piece : (z + 1) * piece]
            f32_ref[at + piece : at + piece + more] = small[z * more : (z + 1) * more]
            f32_ref[at + piece + more : at + chunk] = empty
        out_ref[...] = f32_ref[...].astype(BF)

    return pl.pallas_call(
        kernel,
        out_shape=jax.ShapeDtypeStruct((z_width * chunk, exp_local * slots), BF),
        grid_spec=pltpu.PrefetchScalarGridSpec(
            num_scalar_prefetch=1,
            grid=(exp_local,),
            in_specs=[
                pl.BlockSpec((1, 1, slots), lambda e, c: (e, 0, 0)),
                pl.BlockSpec((1, piece, slots), lambda e, c: (e, 0, 0)),
                pl.BlockSpec((1, task_count, rank, piece), lambda e, c: (e, 0, 0, 0)),
                pl.BlockSpec((1, task_count, rank, width), lambda e, c: (e, 0, 0, 0)),
                pl.BlockSpec((1, z_width, 1, piece, width), lambda e, c: (e, 0, c[0], 0, 0)),
                pl.BlockSpec((1, z_width, piece, width), lambda e, c: (e, 0, 0, 0)),
                pl.BlockSpec((1, slots, width), lambda e, c: (e, 0, 0)),
                pl.BlockSpec((1, slots, width), lambda e, c: (e, 0, 0)),
            ],
            out_specs=pl.BlockSpec((z_width * chunk, slots), lambda e, c: (0, e)),
            scratch_shapes=[pltpu.VMEM((z_width * chunk, slots), F32)],
        ),
        name="partial_sums",
    )(core.reshape(1), task_row, hidden, first, second, weight, weight_peer, rows, rows_peer)


def dispatch_slab(ids, gates, tasks, gradient, expert_count, exp_width, most):
    top, tok_count = ids.shape
    width = gradient.shape[1]
    local = expert_count // exp_width
    slab = local * most
    lines = slab + local + 1
    lines += -lines % 8

    def kernel(id_ref, gate_ref, task_ref, grad_ref, out_ref):
        expert = lax.broadcasted_iota(jnp.int32, (expert_count, tok_count), 0)
        gate = gate_ref[...].astype(F32)
        named = jnp.zeros((expert_count, tok_count), F32)
        weight = jnp.zeros((expert_count, tok_count), F32)
        for k in range(top):
            here = id_ref[k : k + 1] == expert
            named += jnp.where(here, 1.0, 0.0)
            weight += jnp.where(here, gate[k : k + 1], 0.0)
        before = lax.broadcasted_iota(jnp.int32, (tok_count, tok_count), 0)
        after = lax.broadcasted_iota(jnp.int32, (tok_count, tok_count), 1)
        earlier = jnp.where(before < after, 1.0, 0.0).astype(BF)
        place = jnp.dot(named.astype(BF), earlier, preferred_element_type=F32)
        place = jnp.where(named > 0.0, place, -1.0).astype(BF)
        row = lax.broadcasted_iota(jnp.int32, (expert_count * most, expert_count), 0)
        col = lax.broadcasted_iota(jnp.int32, (expert_count * most, expert_count), 1)
        offset = row - col * most
        spread = jnp.where((offset >= 0) & (offset < most), 1.0, 0.0).astype(BF)
        column = lax.broadcasted_iota(jnp.int32, (expert_count, 128), 0)
        place_row = jnp.dot(spread, place, preferred_element_type=F32)
        first = jnp.dot(spread, column.astype(F32).astype(BF), preferred_element_type=F32)
        row_at = lax.broadcasted_iota(jnp.int32, (expert_count * most, tok_count), 0).astype(F32)
        picked = jnp.where(place_row == row_at - first * float(most), 1.0, 0.0).astype(BF)
        rows = jnp.dot(picked, grad_ref[...], preferred_element_type=F32).astype(BF)
        out_ref[:, :slab] = rows.reshape(exp_width, slab, width)
        task = task_ref[...].astype(F32)
        empty = jnp.zeros((lines - slab - local - 1, tok_count), F32)
        for g in range(exp_width):
            tail = [weight[g * local : (g + 1) * local], task, empty]
            out_ref[g, slab:] = jnp.concatenate(tail).astype(BF)

    return pl.pallas_call(
        kernel,
        out_shape=jax.ShapeDtypeStruct((exp_width, lines, width), BF),
        name="dispatch_slab",
    )(ids, gates, tasks, gradient)


def gather_ring(value, axis):
    width = lax.axis_size(axis)
    step = 4

    def ahead(array, shift):
        return lax.ppermute(array, axis, [((i + shift) % width, i) for i in range(width)])

    four = jnp.stack([value, *(ahead(value, step * a) for a in range(1, width // step))])
    parts = [four, ahead(four, 1), ahead(four, 2), ahead(four, -1)]

    def kernel(at_ref, *refs):
        out_ref = refs[-1]
        for shift, ref in zip((0, 1, 2, -1), refs[:-1]):
            for a in range(width // step):
                out_ref[(at_ref[0] + (step * a + shift) % width) % width] = ref[a]

    vmem = pl.BlockSpec(memory_space=pltpu.VMEM)
    return pl.pallas_call(
        kernel,
        out_shape=jax.ShapeDtypeStruct((width, *value.shape), value.dtype),
        in_specs=[pl.BlockSpec(memory_space=pltpu.SMEM)] + [vmem] * len(parts),
        out_specs=vmem,
        name="in_order",
    )(lax.axis_index(axis).astype(jnp.int32).reshape(1), *parts)


def on_device(
    output_gradient,
    routed_expert_index,
    combine,
    token_task_index,
    saved_gate_input,
    saved_up_input,
    down_weight,
    adapter_first_factor,
    adapter_second_factor,
):
    exp_width = lax.axis_size("exp")
    z_width = lax.axis_size("z")
    core = lax.axis_index("core")
    exp_local, source_count, most, piece = saved_gate_input.shape
    tok_count, top = routed_expert_index.shape
    width = output_gradient.shape[1]
    task_count, rank = adapter_first_factor.shape[1], adapter_first_factor.shape[3]
    expert_count = exp_local * exp_width
    per_expert = source_count * most
    total_slots = exp_local * per_expert
    swap = [(0, 1), (1, 0)]

    weight = down_weight.reshape(exp_local, z_width, 2, piece, width)
    weight_peer = lax.ppermute(
        lax.dynamic_index_in_dim(weight, 1 - core, axis=2, keepdims=False), "core", swap
    )

    ids = routed_expert_index.T
    experts = jnp.arange(expert_count, dtype=jnp.int32)
    tokens = jnp.arange(tok_count, dtype=jnp.int32)
    names = ids[:, None, :] == experts[None, :, None]
    named = jnp.any(names, axis=0)
    earlier = (tokens[:, None] < tokens[None, :]).astype(BF)
    place = jnp.dot(named.astype(BF), earlier, preferred_element_type=F32)
    slab = exp_local * most
    send = dispatch_slab(
        ids,
        combine.T,
        token_task_index[None],
        output_gradient,
        expert_count,
        exp_width,
        most,
    )
    received = lax.all_to_all(send, "exp", split_axis=0, concat_axis=0, tiled=True)

    rows = received[:, :slab].transpose(1, 0, 2).reshape(exp_local, per_expert, width)
    rows_peer = lax.ppermute(rows, "core", swap)
    gate_rows = received[:, slab : slab + exp_local].transpose(1, 0, 2)
    used = gate_rows > 0
    place_in = jnp.dot(
        used.astype(BF).reshape(exp_local * source_count, tok_count),
        earlier,
        preferred_element_type=F32,
    ).reshape(exp_local, source_count, tok_count)
    holds = used[:, None] & (
        place_in[:, None] == jnp.arange(most, dtype=jnp.int32).astype(F32)[:, None, None]
    )
    gate_slot = jnp.sum(jnp.where(holds, gate_rows.astype(F32)[:, None], 0.0), axis=3).reshape(
        exp_local, per_expert
    )
    task_rows = received[:, slab + exp_local].astype(F32)
    task_slot = jnp.sum(
        jnp.where(holds, task_rows, 0.0), axis=3
    ).reshape(exp_local, per_expert)
    task_mask = (
        task_slot[:, None] == jnp.arange(task_count, dtype=jnp.int32).astype(F32)[:, None]
    ).astype(F32)

    gate_f = saved_gate_input.transpose(0, 3, 2, 1).reshape(exp_local, piece, per_expert)
    up_f = saved_up_input.transpose(0, 3, 2, 1).reshape(exp_local, piece, per_expert)
    gate_f, up_f = gate_f.astype(F32), up_f.astype(F32)
    sig = jax.nn.sigmoid(gate_f)
    act = gate_f * sig
    hidden = (act * up_f).astype(BF)

    partial = partial_sums(
        core.astype(jnp.int32),
        task_slot[:, None],
        hidden,
        adapter_first_factor.swapaxes(2, 3),
        adapter_second_factor,
        weight,
        weight_peer,
        rows,
        rows_peer,
    )
    summed = lax.psum_scatter(partial, "z", scatter_dimension=0, tiled=True)
    summed = lax.optimization_barrier(summed)
    back = summed[:piece].astype(F32).reshape(piece, exp_local, per_expert).transpose(1, 0, 2)

    pair_part = jnp.sum(hidden.astype(F32) * back, axis=1).reshape(1, total_slots)
    more = 2 * rank // z_width
    small = jnp.concatenate([summed[piece : piece + more], pair_part.astype(BF)])
    small = small.reshape(-1, 128)
    small = small.astype(F32) + lax.ppermute(small, "core", swap).astype(F32)
    everything = gather_ring(small.astype(BF), "z")
    everything = everything.reshape(z_width, more + 1, total_slots)
    split = (rank, exp_local, per_expert)
    latent = everything[: z_width // 2, :more].reshape(split).astype(F32)
    query = everything[z_width // 2 :, :more].reshape(split).astype(F32)
    pair_sum = jnp.sum(everything[:, more].astype(F32), axis=0).reshape(exp_local, per_expert)
    weight_grad = pair_sum + jnp.sum(latent * query, axis=0)

    returned = lax.all_to_all(
        weight_grad.astype(BF).reshape(exp_local, most, source_count).transpose(2, 0, 1),
        "exp",
        split_axis=0,
        concat_axis=0,
        tiled=True,
    ).reshape(expert_count, most)

    scaled = (gate_slot * query).astype(BF)
    spread_update = (
        task_mask.transpose(1, 0, 2)[:, None] * scaled.astype(F32)[None]
    ).astype(BF)
    weighted = (gate_slot * latent).astype(BF)
    spread_z = (task_mask.transpose(1, 0, 2)[:, None] * weighted.astype(F32)[None]).astype(BF)
    first_grad = jnp.einsum(
        "tres,efs->etfr", spread_update, hidden, preferred_element_type=F32
    ).astype(BF)
    second_grad = jnp.einsum(
        "tres,esd->etrd", spread_z, rows, preferred_element_type=F32
    ).astype(BF)
    update_part = jnp.einsum(
        "tres,etfr->efs", spread_update, adapter_first_factor, preferred_element_type=F32
    )
    dh = gate_slot[:, None] * back + update_part
    gate_grad = (dh * up_f * sig * (1.0 + gate_f * (1.0 - sig))).astype(BF)
    up_grad = (dh * act).astype(BF)

    finder = names.transpose(1, 0, 2).reshape(expert_count, top * tok_count).astype(BF)
    place_pick = jnp.sum(jnp.where(names, place[None], 0.0), axis=1).reshape(1, top * tok_count)
    found = jnp.dot(returned.T, finder, preferred_element_type=F32)
    found = jnp.sum(
        jnp.where(jnp.arange(most, dtype=jnp.int32).astype(F32)[:, None] == place_pick, found, 0.0),
        axis=0,
    )
    grad_combine = found.reshape(top, tok_count).T
    shape_out = (exp_local, piece, most, source_count)
    return (
        gate_grad.reshape(shape_out).transpose(0, 3, 2, 1),
        up_grad.reshape(shape_out).transpose(0, 3, 2, 1),
        first_grad,
        second_grad,
        grad_combine,
    )


def solution(mesh):
    exp_width, seq_width = mesh.shape["exp"], mesh.shape["seq"]
    split = Mesh(mesh.devices.reshape(exp_width, seq_width // 2, 2), ("exp", "z", "core"))
    seq = ("z", "core")
    placed = (
        P("exp", seq),
        P("exp", None),
        P("exp", None),
        P("exp"),
        P("exp", None, None, seq),
        P("exp", None, None, seq),
        P("exp", None, seq),
        P("exp", None, seq, None),
        P("exp", None, None, seq),
    )
    return jax.shard_map(
        on_device,
        mesh=split,
        in_specs=placed,
        out_specs=(
            P("exp", None, None, seq),
            P("exp", None, None, seq),
            P("exp", None, seq, None),
            P("exp", None, None, seq),
            P("exp", None),
        ),
        check_vma=False,
    )
```

```python
import jax
import jax.numpy as jnp
from jax import lax
from jax.experimental import pallas as pl
from jax.experimental.pallas import tpu as pltpu
from jax.sharding import Mesh
from jax.sharding import PartitionSpec as P

BF = jnp.bfloat16
F32 = jnp.float32
PAD = 3


def partial_sums(core, task_row, own_pack, peer_pack, second, weight, peer_weight, rows, rows_peer):
    exp_local, z_width, _, piece, width = weight.shape
    slots = rows.shape[1]
    task_count, half = second.shape[1], second.shape[3]
    packed = task_count * half
    more = 2 * half // z_width
    chunk = piece + more + PAD
    first, hidden = own_pack

    def kernel(core_ref, t_ref, a_ref, h_ref, p_ref, b_ref, w_ref, wp_ref, x_ref, xp_ref, out_ref, f32_ref):
        nums = (((1,), (1,)), ((), ()))
        own = w_ref[0, :, 0].reshape(z_width * piece, width)
        peer = wp_ref[0]
        both = jnp.concatenate([x_ref[0], xp_ref[0]], axis=1)
        total = lax.dot_general(
            jnp.concatenate([own, peer[: z_width * piece]], axis=1),
            both,
            nums,
            preferred_element_type=F32,
        )
        ql_all = lax.dot_general(
            jnp.concatenate(
                [b_ref[0, :, 0].reshape(packed, width), peer[z_width * piece :]], axis=1
            ),
            both,
            nums,
            preferred_element_type=F32,
        )
        theirs = p_ref[0]
        lat_all = lax.dot_general(
            jnp.concatenate([a_ref[0, 0], theirs[:, :packed]]),
            jnp.concatenate([h_ref[0], theirs[:, packed:]]),
            (((0,), (0,)), ((), ())),
            preferred_element_type=F32,
        )
        lat = jnp.zeros((half, slots), F32)
        ql = jnp.zeros((half, slots), F32)
        for t in range(task_count):
            keep = t_ref[0] == float(t)
            lat += jnp.where(keep, lat_all[t * half : (t + 1) * half], 0.0)
            ql += jnp.where(keep, ql_all[t * half : (t + 1) * half], 0.0)
        small = jnp.concatenate([lat, ql])
        empty = jnp.zeros((PAD, slots), F32)
        for z in range(z_width):
            at = z * chunk
            f32_ref[at : at + piece] = total[z * piece : (z + 1) * piece]
            f32_ref[at + piece : at + piece + more] = small[z * more : (z + 1) * more]
            f32_ref[at + piece + more : at + chunk] = empty
        out_ref[...] = f32_ref[...].astype(BF)

    return pl.pallas_call(
        kernel,
        out_shape=jax.ShapeDtypeStruct((z_width * chunk, exp_local * slots), BF),
        grid_spec=pltpu.PrefetchScalarGridSpec(
            num_scalar_prefetch=1,
            grid=(exp_local,),
            in_specs=[
                pl.BlockSpec((1, 1, slots), lambda e, c: (e, 0, 0)),
                pl.BlockSpec((1, 1, piece, packed), lambda e, c: (e, c[0], 0, 0)),
                pl.BlockSpec((1, piece, slots), lambda e, c: (e, 0, 0)),
                pl.BlockSpec((1, piece, packed + slots), lambda e, c: (e, 0, 0)),
                pl.BlockSpec((1, task_count, 1, half, width), lambda e, c: (e, 0, c[0], 0, 0)),
                pl.BlockSpec((1, z_width, 1, piece, width), lambda e, c: (e, 0, c[0], 0, 0)),
                pl.BlockSpec((1, z_width * piece + packed, width), lambda e, c: (e, 0, 0)),
                pl.BlockSpec((1, slots, width), lambda e, c: (e, 0, 0)),
                pl.BlockSpec((1, slots, width), lambda e, c: (e, 0, 0)),
            ],
            out_specs=pl.BlockSpec((z_width * chunk, slots), lambda e, c: (0, e)),
            scratch_shapes=[pltpu.VMEM((z_width * chunk, slots), F32)],
        ),
        name="partial_sums",
    )(
        core.reshape(1),
        task_row,
        first,
        hidden,
        peer_pack,
        second,
        weight,
        peer_weight,
        rows,
        rows_peer,
    )


def dispatch_slab(ids, gates, tasks, gradient, expert_count, exp_width, most):
    top, tok_count = ids.shape
    width = gradient.shape[1]
    local = expert_count // exp_width
    slab = local * most
    lines = slab + local + 1
    lines += -lines % 8

    def kernel(id_ref, gate_ref, task_ref, grad_ref, out_ref):
        expert = lax.broadcasted_iota(jnp.int32, (expert_count, tok_count), 0)
        gate = gate_ref[...].astype(F32)
        named = jnp.zeros((expert_count, tok_count), F32)
        weight = jnp.zeros((expert_count, tok_count), F32)
        for k in range(top):
            here = id_ref[k : k + 1] == expert
            named += jnp.where(here, 1.0, 0.0)
            weight += jnp.where(here, gate[k : k + 1], 0.0)
        before = lax.broadcasted_iota(jnp.int32, (tok_count, tok_count), 0)
        after = lax.broadcasted_iota(jnp.int32, (tok_count, tok_count), 1)
        earlier = jnp.where(before < after, 1.0, 0.0).astype(BF)
        place = jnp.dot(named.astype(BF), earlier, preferred_element_type=F32)
        place = jnp.where(named > 0.0, place, -1.0).astype(BF)
        row = lax.broadcasted_iota(jnp.int32, (expert_count * most, expert_count), 0)
        col = lax.broadcasted_iota(jnp.int32, (expert_count * most, expert_count), 1)
        offset = row - col * most
        spread = jnp.where((offset >= 0) & (offset < most), 1.0, 0.0).astype(BF)
        column = lax.broadcasted_iota(jnp.int32, (expert_count, 128), 0)
        place_row = jnp.dot(spread, place, preferred_element_type=F32)
        first = jnp.dot(spread, column.astype(F32).astype(BF), preferred_element_type=F32)
        row_at = lax.broadcasted_iota(jnp.int32, (expert_count * most, tok_count), 0).astype(F32)
        picked = jnp.where(place_row == row_at - first * float(most), 1.0, 0.0).astype(BF)
        rows = jnp.dot(picked, grad_ref[...], preferred_element_type=F32).astype(BF)
        out_ref[:, :slab] = rows.reshape(exp_width, slab, width)
        task = task_ref[...].astype(F32)
        empty = jnp.zeros((lines - slab - local - 1, tok_count), F32)
        for g in range(exp_width):
            tail = [weight[g * local : (g + 1) * local], task, empty]
            out_ref[g, slab:] = jnp.concatenate(tail).astype(BF)

    return pl.pallas_call(
        kernel,
        out_shape=jax.ShapeDtypeStruct((exp_width, lines, width), BF),
        name="dispatch_slab",
    )(ids, gates, tasks, gradient)


def on_device(
    output_gradient,
    routed_expert_index,
    combine,
    token_task_index,
    saved_gate_input,
    saved_up_input,
    down_weight,
    adapter_first_factor,
    adapter_second_factor,
):
    exp_width = lax.axis_size("exp")
    z_width = lax.axis_size("z")
    core = lax.axis_index("core")
    exp_local, source_count, most, piece = saved_gate_input.shape
    tok_count, top = routed_expert_index.shape
    width = output_gradient.shape[1]
    task_count, rank = adapter_first_factor.shape[1], adapter_first_factor.shape[3]
    expert_count = exp_local * exp_width
    per_expert = source_count * most
    total_slots = exp_local * per_expert
    swap = [(0, 1), (1, 0)]

    weight = down_weight.reshape(exp_local, z_width, 2, piece, width)
    half = rank // 2
    second = adapter_second_factor.reshape(exp_local, task_count, 2, half, width)
    first = adapter_first_factor.reshape(exp_local, task_count, piece, 2, half)
    first = first.transpose(0, 3, 2, 1, 4).reshape(exp_local, 2, piece, task_count * half)
    for_peer = [
        lax.dynamic_index_in_dim(a, 1 - core, axis=2, keepdims=False).reshape(exp_local, -1, width)
        for a in (weight, second)
    ]
    peer_weight = lax.ppermute(jnp.concatenate(for_peer, axis=1), "core", swap)

    ids = routed_expert_index.T
    experts = jnp.arange(expert_count, dtype=jnp.int32)
    tokens = jnp.arange(tok_count, dtype=jnp.int32)
    names = ids[:, None, :] == experts[None, :, None]
    named = jnp.any(names, axis=0)
    earlier = (tokens[:, None] < tokens[None, :]).astype(BF)
    place = jnp.dot(named.astype(BF), earlier, preferred_element_type=F32)
    slab = exp_local * most
    send = dispatch_slab(
        ids,
        combine.T,
        token_task_index[None],
        output_gradient,
        expert_count,
        exp_width,
        most,
    )
    received = lax.all_to_all(send, "exp", split_axis=0, concat_axis=0, tiled=True)

    rows = received[:, :slab].transpose(1, 0, 2).reshape(exp_local, per_expert, width)
    rows_peer = lax.ppermute(rows, "core", swap)
    gate_rows = received[:, slab : slab + exp_local].transpose(1, 0, 2)
    used = gate_rows > 0
    place_in = jnp.dot(
        used.astype(BF).reshape(exp_local * source_count, tok_count),
        earlier,
        preferred_element_type=F32,
    ).reshape(exp_local, source_count, tok_count)
    holds = used[:, None] & (
        place_in[:, None] == jnp.arange(most, dtype=jnp.int32).astype(F32)[:, None, None]
    )
    gate_slot = jnp.sum(jnp.where(holds, gate_rows.astype(F32)[:, None], 0.0), axis=3).reshape(
        exp_local, per_expert
    )
    task_rows = received[:, slab + exp_local].astype(F32)
    task_slot = jnp.sum(
        jnp.where(holds, task_rows, 0.0), axis=3
    ).reshape(exp_local, per_expert)
    task_mask = (
        task_slot[:, None] == jnp.arange(task_count, dtype=jnp.int32).astype(F32)[:, None]
    ).astype(F32)

    gate_f = saved_gate_input.transpose(0, 3, 2, 1).reshape(exp_local, piece, per_expert)
    up_f = saved_up_input.transpose(0, 3, 2, 1).reshape(exp_local, piece, per_expert)
    gate_f, up_f = gate_f.astype(F32), up_f.astype(F32)
    sig = jax.nn.sigmoid(gate_f)
    act = gate_f * sig
    hidden = (act * up_f).astype(BF)

    first_send = lax.dynamic_index_in_dim(first, 1 - core, axis=1, keepdims=False)
    peer_pack = lax.ppermute(jnp.concatenate([first_send, hidden], axis=2), "core", swap)

    partial = partial_sums(
        core.astype(jnp.int32),
        task_slot[:, None],
        (first, hidden),
        peer_pack,
        second,
        weight,
        peer_weight,
        rows,
        rows_peer,
    )
    summed = lax.psum_scatter(partial, "z", scatter_dimension=0, tiled=True)
    summed = lax.optimization_barrier(summed)
    back = summed[:piece].astype(F32).reshape(piece, exp_local, per_expert).transpose(1, 0, 2)

    pair_part = jnp.sum(hidden.astype(F32) * back, axis=1).reshape(1, total_slots)
    more = 2 * half // z_width
    small = jnp.concatenate([summed[piece : piece + more], pair_part.astype(BF)])
    gathered = lax.all_gather(small.reshape(-1, 128), "z", axis=0, tiled=False)
    sides = []
    for side in (gathered, lax.ppermute(gathered, "core", swap)):
        side = side.reshape(z_width, more + 1, total_slots).astype(F32)
        lat_side = side[: z_width // 2, :more].reshape(half, exp_local, per_expert)
        ql_side = side[z_width // 2 :, :more].reshape(half, exp_local, per_expert)
        sums = jnp.sum(side[:, more], axis=0).reshape(exp_local, per_expert)
        sides.append((lat_side, ql_side, sums + jnp.sum(lat_side * ql_side, axis=0)))
    own_side, peer_side = sides
    weight_grad = own_side[2] + peer_side[2]
    latent, query = (
        jnp.where(core == 0, jnp.concatenate([a, b]), jnp.concatenate([b, a]))
        for a, b in zip(own_side[:2], peer_side[:2])
    )

    returned = lax.all_to_all(
        weight_grad.astype(BF).reshape(exp_local, most, source_count).transpose(2, 0, 1),
        "exp",
        split_axis=0,
        concat_axis=0,
        tiled=True,
    ).reshape(expert_count, most)

    scaled = (gate_slot * query).astype(BF)
    spread_update = (
        task_mask.transpose(1, 0, 2)[:, None] * scaled.astype(F32)[None]
    ).astype(BF)
    weighted = (gate_slot * latent).astype(BF)
    spread_z = (task_mask.transpose(1, 0, 2)[:, None] * weighted.astype(F32)[None]).astype(BF)
    first_grad = jnp.einsum(
        "tres,efs->etfr", spread_update, hidden, preferred_element_type=F32
    ).astype(BF)
    second_grad = jnp.einsum(
        "tres,esd->etrd", spread_z, rows, preferred_element_type=F32
    ).astype(BF)
    update_part = jnp.einsum(
        "tres,etfr->efs", spread_update, adapter_first_factor, preferred_element_type=F32
    )
    dh = gate_slot[:, None] * back + update_part
    gate_grad = (dh * up_f * sig * (1.0 + gate_f * (1.0 - sig))).astype(BF)
    up_grad = (dh * act).astype(BF)

    finder = names.transpose(1, 0, 2).reshape(expert_count, top * tok_count).astype(BF)
    place_pick = jnp.sum(jnp.where(names, place[None], 0.0), axis=1).reshape(1, top * tok_count)
    found = jnp.dot(returned.T, finder, preferred_element_type=F32)
    found = jnp.sum(
        jnp.where(jnp.arange(most, dtype=jnp.int32).astype(F32)[:, None] == place_pick, found, 0.0),
        axis=0,
    )
    grad_combine = found.reshape(top, tok_count).T
    shape_out = (exp_local, piece, most, source_count)
    return (
        gate_grad.reshape(shape_out).transpose(0, 3, 2, 1),
        up_grad.reshape(shape_out).transpose(0, 3, 2, 1),
        first_grad,
        second_grad,
        grad_combine,
    )


def solution(mesh):
    exp_width, seq_width = mesh.shape["exp"], mesh.shape["seq"]
    split = Mesh(mesh.devices.reshape(exp_width, seq_width // 2, 2), ("exp", "z", "core"))
    seq = ("z", "core")
    placed = (
        P("exp", seq),
        P("exp", None),
        P("exp", None),
        P("exp"),
        P("exp", None, None, seq),
        P("exp", None, None, seq),
        P("exp", None, seq),
        P("exp", None, seq, None),
        P("exp", None, None, seq),
    )
    return jax.shard_map(
        on_device,
        mesh=split,
        in_specs=placed,
        out_specs=(
            P("exp", None, None, seq),
            P("exp", None, None, seq),
            P("exp", None, seq, None),
            P("exp", None, None, seq),
            P("exp", None),
        ),
        check_vma=False,
    )
```

```python
import jax
import jax.numpy as jnp
from jax import lax
from jax.experimental import pallas as pl
from jax.experimental.pallas import tpu as pltpu
from jax.sharding import Mesh
from jax.sharding import PartitionSpec as P

BF = jnp.bfloat16
F32 = jnp.float32
PAD = 3


def partial_sums(core, task_row, own_pack, peer_pack, second, weight, peer_weight, rows, rows_peer):
    exp_local, z_width, _, piece, width = weight.shape
    slots = rows.shape[1]
    task_count, half = second.shape[1], second.shape[3]
    packed = task_count * half
    more = 2 * half // z_width
    chunk = piece + more + PAD
    first, hidden = own_pack

    def kernel(core_ref, t_ref, a_ref, h_ref, p_ref, b_ref, w_ref, wp_ref, x_ref, xp_ref, out_ref, f32_ref):
        nums = (((1,), (1,)), ((), ()))
        own = w_ref[0, :, 0].reshape(z_width * piece, width)
        peer = wp_ref[0]
        both = jnp.concatenate([x_ref[0], xp_ref[0]], axis=1)
        total = lax.dot_general(
            jnp.concatenate([own, peer[: z_width * piece]], axis=1),
            both,
            nums,
            preferred_element_type=F32,
        )
        ql_all = lax.dot_general(
            jnp.concatenate(
                [b_ref[0, :, 0].reshape(packed, width), peer[z_width * piece :]], axis=1
            ),
            both,
            nums,
            preferred_element_type=F32,
        )
        theirs = p_ref[0]
        lat_all = lax.dot_general(
            jnp.concatenate([a_ref[0, 0], theirs[:, :packed]]),
            jnp.concatenate([h_ref[0], theirs[:, packed:]]),
            (((0,), (0,)), ((), ())),
            preferred_element_type=F32,
        )
        lat = jnp.zeros((half, slots), F32)
        ql = jnp.zeros((half, slots), F32)
        for t in range(task_count):
            keep = t_ref[0] == float(t)
            lat += jnp.where(keep, lat_all[t * half : (t + 1) * half], 0.0)
            ql += jnp.where(keep, ql_all[t * half : (t + 1) * half], 0.0)
        small = jnp.concatenate([lat, ql])
        empty = jnp.zeros((PAD, slots), F32)
        for z in range(z_width):
            at = z * chunk
            f32_ref[at : at + piece] = total[z * piece : (z + 1) * piece]
            f32_ref[at + piece : at + piece + more] = small[z * more : (z + 1) * more]
            f32_ref[at + piece + more : at + chunk] = empty
        out_ref[...] = f32_ref[...].astype(BF)

    return pl.pallas_call(
        kernel,
        out_shape=jax.ShapeDtypeStruct((z_width * chunk, exp_local * slots), BF),
        grid_spec=pltpu.PrefetchScalarGridSpec(
            num_scalar_prefetch=1,
            grid=(exp_local,),
            in_specs=[
                pl.BlockSpec((1, 1, slots), lambda e, c: (e, 0, 0)),
                pl.BlockSpec((1, 1, piece, packed), lambda e, c: (e, c[0], 0, 0)),
                pl.BlockSpec((1, piece, slots), lambda e, c: (e, 0, 0)),
                pl.BlockSpec((1, piece, packed + slots), lambda e, c: (e, 0, 0)),
                pl.BlockSpec((1, task_count, 1, half, width), lambda e, c: (e, 0, c[0], 0, 0)),
                pl.BlockSpec((1, z_width, 1, piece, width), lambda e, c: (e, 0, c[0], 0, 0)),
                pl.BlockSpec((1, z_width * piece + packed, width), lambda e, c: (e, 0, 0)),
                pl.BlockSpec((1, slots, width), lambda e, c: (e, 0, 0)),
                pl.BlockSpec((1, slots, width), lambda e, c: (e, 0, 0)),
            ],
            out_specs=pl.BlockSpec((z_width * chunk, slots), lambda e, c: (0, e)),
            scratch_shapes=[pltpu.VMEM((z_width * chunk, slots), F32)],
        ),
        name="partial_sums",
    )(
        core.reshape(1),
        task_row,
        first,
        hidden,
        peer_pack,
        second,
        weight,
        peer_weight,
        rows,
        rows_peer,
    )


def dispatch_slab(ids, gates, tasks, gradient, expert_count, exp_width, most):
    top, tok_count = ids.shape
    width = gradient.shape[1]
    local = expert_count // exp_width
    slab = local * most
    lines = slab + local + 1
    lines += -lines % 8

    def kernel(id_ref, gate_ref, task_ref, grad_ref, out_ref):
        expert = lax.broadcasted_iota(jnp.int32, (expert_count, tok_count), 0)
        gate = gate_ref[...].astype(F32)
        named = jnp.zeros((expert_count, tok_count), F32)
        weight = jnp.zeros((expert_count, tok_count), F32)
        for k in range(top):
            here = id_ref[k : k + 1] == expert
            named += jnp.where(here, 1.0, 0.0)
            weight += jnp.where(here, gate[k : k + 1], 0.0)
        before = lax.broadcasted_iota(jnp.int32, (tok_count, tok_count), 0)
        after = lax.broadcasted_iota(jnp.int32, (tok_count, tok_count), 1)
        earlier = jnp.where(before < after, 1.0, 0.0).astype(BF)
        place = jnp.dot(named.astype(BF), earlier, preferred_element_type=F32)
        place = jnp.where(named > 0.0, place, -1.0).astype(BF)
        row = lax.broadcasted_iota(jnp.int32, (expert_count * most, expert_count), 0)
        col = lax.broadcasted_iota(jnp.int32, (expert_count * most, expert_count), 1)
        offset = row - col * most
        spread = jnp.where((offset >= 0) & (offset < most), 1.0, 0.0).astype(BF)
        column = lax.broadcasted_iota(jnp.int32, (expert_count, 128), 0)
        place_row = jnp.dot(spread, place, preferred_element_type=F32)
        first = jnp.dot(spread, column.astype(F32).astype(BF), preferred_element_type=F32)
        row_at = lax.broadcasted_iota(jnp.int32, (expert_count * most, tok_count), 0).astype(F32)
        picked = jnp.where(place_row == row_at - first * float(most), 1.0, 0.0).astype(BF)
        rows = jnp.dot(picked, grad_ref[...], preferred_element_type=F32).astype(BF)
        out_ref[:, :slab] = rows.reshape(exp_width, slab, width)
        task = task_ref[...].astype(F32)
        empty = jnp.zeros((lines - slab - local - 1, tok_count), F32)
        for g in range(exp_width):
            tail = [weight[g * local : (g + 1) * local], task, empty]
            out_ref[g, slab:] = jnp.concatenate(tail).astype(BF)

    return pl.pallas_call(
        kernel,
        out_shape=jax.ShapeDtypeStruct((exp_width, lines, width), BF),
        name="dispatch_slab",
    )(ids, gates, tasks, gradient)


def on_device(
    output_gradient,
    routed_expert_index,
    combine,
    token_task_index,
    saved_gate_input,
    saved_up_input,
    down_weight,
    adapter_first_factor,
    adapter_second_factor,
):
    exp_width = lax.axis_size("exp")
    z_width = lax.axis_size("z")
    core = lax.axis_index("core")
    exp_local, source_count, most, piece = saved_gate_input.shape
    tok_count, top = routed_expert_index.shape
    width = output_gradient.shape[1]
    task_count, rank = adapter_first_factor.shape[1], adapter_first_factor.shape[3]
    expert_count = exp_local * exp_width
    per_expert = source_count * most
    total_slots = exp_local * per_expert
    swap = [(0, 1), (1, 0)]

    weight = down_weight.reshape(exp_local, z_width, 2, piece, width)
    half = rank // 2
    second = adapter_second_factor.reshape(exp_local, task_count, 2, half, width)
    first = adapter_first_factor.reshape(exp_local, task_count, piece, 2, half)
    first = first.transpose(0, 3, 2, 1, 4).reshape(exp_local, 2, piece, task_count * half)
    for_peer = [
        lax.dynamic_index_in_dim(a, 1 - core, axis=2, keepdims=False).reshape(exp_local, -1, width)
        for a in (weight, second)
    ]
    peer_weight = lax.ppermute(jnp.concatenate(for_peer, axis=1), "core", swap)

    ids = routed_expert_index.T
    experts = jnp.arange(expert_count, dtype=jnp.int32)
    tokens = jnp.arange(tok_count, dtype=jnp.int32)
    names = ids[:, None, :] == experts[None, :, None]
    named = jnp.any(names, axis=0)
    earlier = (tokens[:, None] < tokens[None, :]).astype(BF)
    place = jnp.dot(named.astype(BF), earlier, preferred_element_type=F32)
    slab = exp_local * most
    send = dispatch_slab(
        ids,
        combine.T,
        token_task_index[None],
        output_gradient,
        expert_count,
        exp_width,
        most,
    )
    received = lax.all_to_all(send, "exp", split_axis=0, concat_axis=0, tiled=True)

    rows = received[:, :slab].transpose(1, 0, 2).reshape(exp_local, per_expert, width)
    rows_peer = lax.ppermute(rows, "core", swap)
    gate_rows = received[:, slab : slab + exp_local].transpose(1, 0, 2)
    used = gate_rows > 0
    place_in = jnp.dot(
        used.astype(BF).reshape(exp_local * source_count, tok_count),
        earlier,
        preferred_element_type=F32,
    ).reshape(exp_local, source_count, tok_count)
    holds = used[:, None] & (
        place_in[:, None] == jnp.arange(most, dtype=jnp.int32).astype(F32)[:, None, None]
    )
    gate_slot = jnp.sum(jnp.where(holds, gate_rows.astype(F32)[:, None], 0.0), axis=3).reshape(
        exp_local, per_expert
    )
    task_rows = received[:, slab + exp_local].astype(F32)
    task_slot = jnp.sum(
        jnp.where(holds, task_rows, 0.0), axis=3
    ).reshape(exp_local, per_expert)
    task_mask = (
        task_slot[:, None] == jnp.arange(task_count, dtype=jnp.int32).astype(F32)[:, None]
    ).astype(F32)

    gate_f = saved_gate_input.transpose(0, 3, 2, 1).reshape(exp_local, piece, per_expert)
    up_f = saved_up_input.transpose(0, 3, 2, 1).reshape(exp_local, piece, per_expert)
    gate_f, up_f = gate_f.astype(F32), up_f.astype(F32)
    sig = jax.nn.sigmoid(gate_f)
    act = gate_f * sig
    hidden = (act * up_f).astype(BF)

    first_send = lax.dynamic_index_in_dim(first, 1 - core, axis=1, keepdims=False)
    peer_pack = lax.ppermute(jnp.concatenate([first_send, hidden], axis=2), "core", swap)

    partial = partial_sums(
        core.astype(jnp.int32),
        task_slot[:, None],
        (first, hidden),
        peer_pack,
        second,
        weight,
        peer_weight,
        rows,
        rows_peer,
    )
    summed = lax.psum_scatter(partial, "z", scatter_dimension=0, tiled=True)
    summed = lax.optimization_barrier(summed)
    back = summed[:piece].astype(F32).reshape(piece, exp_local, per_expert).transpose(1, 0, 2)

    pair_part = jnp.sum(hidden.astype(F32) * back, axis=1).reshape(1, total_slots)
    more = 2 * half // z_width
    small = jnp.concatenate([summed[piece : piece + more], pair_part.astype(BF)])
    rings = [[2 * z + (z + p) % 2 for z in range(z_width)] for p in range(2)]
    gathered = lax.all_gather(
        small.reshape(-1, 128), ("z", "core"), axis=0, tiled=False, axis_index_groups=rings
    )
    sides = []
    for side in (gathered, lax.ppermute(gathered, "core", swap)):
        side = side.reshape(z_width, more + 1, total_slots).astype(F32)
        lat_side, ql_side = side[: z_width // 2, :more], side[z_width // 2 :, :more]
        sums = jnp.sum(side[:, more], axis=0) + jnp.sum(lat_side * ql_side, axis=(0, 1))
        sides.append((lat_side, ql_side, sums.reshape(exp_local, per_expert)))
    own_side, peer_side = sides
    weight_grad = own_side[2] + peer_side[2]
    from_core = (lax.axis_index("z") + core + jnp.arange(z_width // 2, dtype=jnp.int32)) % 2
    from_core = from_core[:, None, None]
    latent, query = (
        jnp.concatenate(
            [jnp.where(from_core == 0, a, b), jnp.where(from_core == 0, b, a)]
        ).reshape(rank, exp_local, per_expert)
        for a, b in zip(own_side[:2], peer_side[:2])
    )

    returned = lax.all_to_all(
        weight_grad.astype(BF).reshape(exp_local, most, source_count).transpose(2, 0, 1),
        "exp",
        split_axis=0,
        concat_axis=0,
        tiled=True,
    ).reshape(expert_count, most)

    scaled = (gate_slot * query).astype(BF)
    spread_update = (
        task_mask.transpose(1, 0, 2)[:, None] * scaled.astype(F32)[None]
    ).astype(BF)
    weighted = (gate_slot * latent).astype(BF)
    spread_z = (task_mask.transpose(1, 0, 2)[:, None] * weighted.astype(F32)[None]).astype(BF)
    first_grad = jnp.einsum(
        "tres,efs->etfr", spread_update, hidden, preferred_element_type=F32
    ).astype(BF)
    second_grad = jnp.einsum(
        "tres,esd->etrd", spread_z, rows, preferred_element_type=F32
    ).astype(BF)
    update_part = jnp.einsum(
        "tres,etfr->efs", spread_update, adapter_first_factor, preferred_element_type=F32
    )
    dh = gate_slot[:, None] * back + update_part
    gate_grad = (dh * up_f * sig * (1.0 + gate_f * (1.0 - sig))).astype(BF)
    up_grad = (dh * act).astype(BF)

    finder = names.transpose(1, 0, 2).reshape(expert_count, top * tok_count).astype(BF)
    place_pick = jnp.sum(jnp.where(names, place[None], 0.0), axis=1).reshape(1, top * tok_count)
    found = jnp.dot(returned.T, finder, preferred_element_type=F32)
    found = jnp.sum(
        jnp.where(jnp.arange(most, dtype=jnp.int32).astype(F32)[:, None] == place_pick, found, 0.0),
        axis=0,
    )
    grad_combine = found.reshape(top, tok_count).T
    shape_out = (exp_local, piece, most, source_count)
    return (
        gate_grad.reshape(shape_out).transpose(0, 3, 2, 1),
        up_grad.reshape(shape_out).transpose(0, 3, 2, 1),
        first_grad,
        second_grad,
        grad_combine,
    )


def solution(mesh):
    exp_width, seq_width = mesh.shape["exp"], mesh.shape["seq"]
    split = Mesh(mesh.devices.reshape(exp_width, seq_width // 2, 2), ("exp", "z", "core"))
    seq = ("z", "core")
    placed = (
        P("exp", seq),
        P("exp", None),
        P("exp", None),
        P("exp"),
        P("exp", None, None, seq),
        P("exp", None, None, seq),
        P("exp", None, seq),
        P("exp", None, seq, None),
        P("exp", None, None, seq),
    )
    return jax.shard_map(
        on_device,
        mesh=split,
        in_specs=placed,
        out_specs=(
            P("exp", None, None, seq),
            P("exp", None, None, seq),
            P("exp", None, seq, None),
            P("exp", None, None, seq),
            P("exp", None),
        ),
        check_vma=False,
    )
```

```python
import jax
import jax.numpy as jnp
from jax import lax
from jax.experimental import pallas as pl
from jax.experimental.pallas import tpu as pltpu
from jax.sharding import Mesh
from jax.sharding import PartitionSpec as P

BF = jnp.bfloat16
F32 = jnp.float32
PAD = 3


def partial_sums(core, task_row, own_pack, peer_pack, second, weight, peer_weight, rows, rows_peer):
    exp_local, z_width, _, piece, width = weight.shape
    slots = rows.shape[1]
    task_count, half = second.shape[1], second.shape[3]
    packed = task_count * half
    more = 2 * half // z_width
    chunk = piece + more + PAD
    first, hidden = own_pack

    def kernel(core_ref, t_ref, a_ref, h_ref, p_ref, b_ref, w_ref, wp_ref, x_ref, xp_ref, out_ref, f32_ref):
        nums = (((1,), (1,)), ((), ()))
        own = jnp.concatenate([w_ref[0, z, (core_ref[0] + z) % 2] for z in range(z_width)])
        peer = wp_ref[0]
        both = jnp.concatenate([x_ref[0], xp_ref[0]], axis=1)
        total = lax.dot_general(
            jnp.concatenate([own, peer[: z_width * piece]], axis=1),
            both,
            nums,
            preferred_element_type=F32,
        )
        ql_all = lax.dot_general(
            jnp.concatenate(
                [b_ref[0, :, 0].reshape(packed, width), peer[z_width * piece :]], axis=1
            ),
            both,
            nums,
            preferred_element_type=F32,
        )
        theirs = p_ref[0]
        lat_all = lax.dot_general(
            jnp.concatenate([a_ref[0, 0], theirs[:, :packed]]),
            jnp.concatenate([h_ref[0], theirs[:, packed:]]),
            (((0,), (0,)), ((), ())),
            preferred_element_type=F32,
        )
        lat = jnp.zeros((half, slots), F32)
        ql = jnp.zeros((half, slots), F32)
        for t in range(task_count):
            keep = t_ref[0] == float(t)
            lat += jnp.where(keep, lat_all[t * half : (t + 1) * half], 0.0)
            ql += jnp.where(keep, ql_all[t * half : (t + 1) * half], 0.0)
        small = jnp.concatenate([lat, ql])
        empty = jnp.zeros((PAD, slots), F32)
        for z in range(z_width):
            at = z * chunk
            f32_ref[at : at + piece] = total[z * piece : (z + 1) * piece]
            f32_ref[at + piece : at + piece + more] = small[z * more : (z + 1) * more]
            f32_ref[at + piece + more : at + chunk] = empty
        out_ref[...] = f32_ref[...].astype(BF)

    return pl.pallas_call(
        kernel,
        out_shape=jax.ShapeDtypeStruct((z_width * chunk, exp_local * slots), BF),
        grid_spec=pltpu.PrefetchScalarGridSpec(
            num_scalar_prefetch=1,
            grid=(exp_local,),
            in_specs=[
                pl.BlockSpec((1, 1, slots), lambda e, c: (e, 0, 0)),
                pl.BlockSpec((1, 1, piece, packed), lambda e, c: (e, c[0], 0, 0)),
                pl.BlockSpec((1, piece, slots), lambda e, c: (e, 0, 0)),
                pl.BlockSpec((1, piece, packed + slots), lambda e, c: (e, 0, 0)),
                pl.BlockSpec((1, task_count, 1, half, width), lambda e, c: (e, 0, c[0], 0, 0)),
                pl.BlockSpec((1, z_width, 2, piece, width), lambda e, c: (e, 0, 0, 0, 0)),
                pl.BlockSpec((1, z_width * piece + packed, width), lambda e, c: (e, 0, 0)),
                pl.BlockSpec((1, slots, width), lambda e, c: (e, 0, 0)),
                pl.BlockSpec((1, slots, width), lambda e, c: (e, 0, 0)),
            ],
            out_specs=pl.BlockSpec((z_width * chunk, slots), lambda e, c: (0, e)),
            scratch_shapes=[pltpu.VMEM((z_width * chunk, slots), F32)],
        ),
        name="partial_sums",
    )(
        core.reshape(1),
        task_row,
        first,
        hidden,
        peer_pack,
        second,
        weight,
        peer_weight,
        rows,
        rows_peer,
    )


def dispatch_slab(ids, gates, tasks, gradient, expert_count, exp_width, most):
    top, tok_count = ids.shape
    width = gradient.shape[1]
    local = expert_count // exp_width
    slab = local * most
    lines = slab + local + 1
    lines += -lines % 8

    def kernel(id_ref, gate_ref, task_ref, grad_ref, out_ref):
        expert = lax.broadcasted_iota(jnp.int32, (expert_count, tok_count), 0)
        gate = gate_ref[...].astype(F32)
        named = jnp.zeros((expert_count, tok_count), F32)
        weight = jnp.zeros((expert_count, tok_count), F32)
        for k in range(top):
            here = id_ref[k : k + 1] == expert
            named += jnp.where(here, 1.0, 0.0)
            weight += jnp.where(here, gate[k : k + 1], 0.0)
        before = lax.broadcasted_iota(jnp.int32, (tok_count, tok_count), 0)
        after = lax.broadcasted_iota(jnp.int32, (tok_count, tok_count), 1)
        earlier = jnp.where(before < after, 1.0, 0.0).astype(BF)
        place = jnp.dot(named.astype(BF), earlier, preferred_element_type=F32)
        place = jnp.where(named > 0.0, place, -1.0).astype(BF)
        row = lax.broadcasted_iota(jnp.int32, (expert_count * most, expert_count), 0)
        col = lax.broadcasted_iota(jnp.int32, (expert_count * most, expert_count), 1)
        offset = row - col * most
        spread = jnp.where((offset >= 0) & (offset < most), 1.0, 0.0).astype(BF)
        column = lax.broadcasted_iota(jnp.int32, (expert_count, 128), 0)
        place_row = jnp.dot(spread, place, preferred_element_type=F32)
        first = jnp.dot(spread, column.astype(F32).astype(BF), preferred_element_type=F32)
        row_at = lax.broadcasted_iota(jnp.int32, (expert_count * most, tok_count), 0).astype(F32)
        picked = jnp.where(place_row == row_at - first * float(most), 1.0, 0.0).astype(BF)
        rows = jnp.dot(picked, grad_ref[...], preferred_element_type=F32).astype(BF)
        out_ref[:, :slab] = rows.reshape(exp_width, slab, width)
        task = task_ref[...].astype(F32)
        empty = jnp.zeros((lines - slab - local - 1, tok_count), F32)
        for g in range(exp_width):
            tail = [weight[g * local : (g + 1) * local], task, empty]
            out_ref[g, slab:] = jnp.concatenate(tail).astype(BF)

    return pl.pallas_call(
        kernel,
        out_shape=jax.ShapeDtypeStruct((exp_width, lines, width), BF),
        name="dispatch_slab",
    )(ids, gates, tasks, gradient)


def on_device(
    output_gradient,
    routed_expert_index,
    combine,
    token_task_index,
    saved_gate_input,
    saved_up_input,
    down_weight,
    adapter_first_factor,
    adapter_second_factor,
):
    exp_width = lax.axis_size("exp")
    z_width = lax.axis_size("z")
    core = lax.axis_index("core")
    exp_local, source_count, most, piece = saved_gate_input.shape
    tok_count, top = routed_expert_index.shape
    width = output_gradient.shape[1]
    task_count, rank = adapter_first_factor.shape[1], adapter_first_factor.shape[3]
    expert_count = exp_local * exp_width
    per_expert = source_count * most
    total_slots = exp_local * per_expert
    swap = [(0, 1), (1, 0)]

    weight = down_weight.reshape(exp_local, z_width, 2, piece, width)
    half = rank // 2
    second = adapter_second_factor.reshape(exp_local, task_count, 2, half, width)
    first = adapter_first_factor.reshape(exp_local, task_count, piece, 2, half)
    first = first.transpose(0, 3, 2, 1, 4).reshape(exp_local, 2, piece, task_count * half)
    ring = (lax.axis_index("z") + core) % 2
    rings = [[2 * z + (z + p) % 2 for z in range(z_width)] for p in range(2)]
    to_core = (jnp.arange(z_width, dtype=jnp.int32) + ring) % 2
    for_peer = [
        jnp.where(to_core[:, None, None] == 0, weight[:, :, 1], weight[:, :, 0]),
        lax.dynamic_index_in_dim(second, 1 - ring, axis=2, keepdims=False),
    ]
    for_peer = [a.reshape(exp_local, -1, width) for a in for_peer]
    peer_weight = lax.ppermute(jnp.concatenate(for_peer, axis=1), "core", swap)

    ids = routed_expert_index.T
    experts = jnp.arange(expert_count, dtype=jnp.int32)
    tokens = jnp.arange(tok_count, dtype=jnp.int32)
    names = ids[:, None, :] == experts[None, :, None]
    named = jnp.any(names, axis=0)
    earlier = (tokens[:, None] < tokens[None, :]).astype(BF)
    place = jnp.dot(named.astype(BF), earlier, preferred_element_type=F32)
    slab = exp_local * most
    send = dispatch_slab(
        ids,
        combine.T,
        token_task_index[None],
        output_gradient,
        expert_count,
        exp_width,
        most,
    )
    received = lax.all_to_all(send, "exp", split_axis=0, concat_axis=0, tiled=True)

    rows = received[:, :slab].transpose(1, 0, 2).reshape(exp_local, per_expert, width)
    rows_peer = lax.ppermute(rows, "core", swap)
    gate_rows = received[:, slab : slab + exp_local].transpose(1, 0, 2)
    used = gate_rows > 0
    place_in = jnp.dot(
        used.astype(BF).reshape(exp_local * source_count, tok_count),
        earlier,
        preferred_element_type=F32,
    ).reshape(exp_local, source_count, tok_count)
    holds = used[:, None] & (
        place_in[:, None] == jnp.arange(most, dtype=jnp.int32).astype(F32)[:, None, None]
    )
    gate_slot = jnp.sum(jnp.where(holds, gate_rows.astype(F32)[:, None], 0.0), axis=3).reshape(
        exp_local, per_expert
    )
    task_rows = received[:, slab + exp_local].astype(F32)
    task_slot = jnp.sum(
        jnp.where(holds, task_rows, 0.0), axis=3
    ).reshape(exp_local, per_expert)
    task_mask = (
        task_slot[:, None] == jnp.arange(task_count, dtype=jnp.int32).astype(F32)[:, None]
    ).astype(F32)

    gate_f = saved_gate_input.transpose(0, 3, 2, 1).reshape(exp_local, piece, per_expert)
    up_f = saved_up_input.transpose(0, 3, 2, 1).reshape(exp_local, piece, per_expert)
    gate_f, up_f = gate_f.astype(F32), up_f.astype(F32)
    sig = jax.nn.sigmoid(gate_f)
    act = gate_f * sig
    hidden = (act * up_f).astype(BF)

    first_send = lax.dynamic_index_in_dim(first, 1 - ring, axis=1, keepdims=False)
    peer_pack = lax.ppermute(jnp.concatenate([first_send, hidden], axis=2), "core", swap)

    partial = partial_sums(
        ring.astype(jnp.int32),
        task_slot[:, None],
        (first, hidden),
        peer_pack,
        second,
        weight,
        peer_weight,
        rows,
        rows_peer,
    )
    summed = lax.psum_scatter(
        partial, ("z", "core"), scatter_dimension=0, tiled=True, axis_index_groups=rings
    )
    summed = lax.optimization_barrier(summed)
    back = summed[:piece].astype(F32).reshape(piece, exp_local, per_expert).transpose(1, 0, 2)

    pair_part = jnp.sum(hidden.astype(F32) * back, axis=1).reshape(1, total_slots)
    more = 2 * half // z_width
    small = jnp.concatenate([summed[piece : piece + more], pair_part.astype(BF)])
    gathered = lax.all_gather(
        small.reshape(-1, 128), ("z", "core"), axis=0, tiled=False, axis_index_groups=rings
    )
    sides = []
    for side in (gathered, lax.ppermute(gathered, "core", swap)):
        side = side.reshape(z_width, more + 1, total_slots).astype(F32)
        lat_side, ql_side = side[: z_width // 2, :more], side[z_width // 2 :, :more]
        sums = jnp.sum(side[:, more], axis=0) + jnp.sum(lat_side * ql_side, axis=(0, 1))
        sides.append((lat_side, ql_side, sums.reshape(exp_local, per_expert)))
    own_side, peer_side = sides
    weight_grad = own_side[2] + peer_side[2]
    latent, query = (
        jnp.where(ring == 0, jnp.concatenate([a, b]), jnp.concatenate([b, a])).reshape(
            rank, exp_local, per_expert
        )
        for a, b in zip(own_side[:2], peer_side[:2])
    )

    returned = lax.all_to_all(
        weight_grad.astype(BF).reshape(exp_local, most, source_count).transpose(2, 0, 1),
        "exp",
        split_axis=0,
        concat_axis=0,
        tiled=True,
    ).reshape(expert_count, most)

    scaled = (gate_slot * query).astype(BF)
    spread_update = (
        task_mask.transpose(1, 0, 2)[:, None] * scaled.astype(F32)[None]
    ).astype(BF)
    weighted = (gate_slot * latent).astype(BF)
    spread_z = (task_mask.transpose(1, 0, 2)[:, None] * weighted.astype(F32)[None]).astype(BF)
    first_grad = jnp.einsum(
        "tres,efs->etfr", spread_update, hidden, preferred_element_type=F32
    ).astype(BF)
    second_grad = jnp.einsum(
        "tres,esd->etrd", spread_z, rows, preferred_element_type=F32
    ).astype(BF)
    update_part = jnp.einsum(
        "tres,etfr->efs", spread_update, adapter_first_factor, preferred_element_type=F32
    )
    dh = gate_slot[:, None] * back + update_part
    gate_grad = (dh * up_f * sig * (1.0 + gate_f * (1.0 - sig))).astype(BF)
    up_grad = (dh * act).astype(BF)

    finder = names.transpose(1, 0, 2).reshape(expert_count, top * tok_count).astype(BF)
    place_pick = jnp.sum(jnp.where(names, place[None], 0.0), axis=1).reshape(1, top * tok_count)
    found = jnp.dot(returned.T, finder, preferred_element_type=F32)
    found = jnp.sum(
        jnp.where(jnp.arange(most, dtype=jnp.int32).astype(F32)[:, None] == place_pick, found, 0.0),
        axis=0,
    )
    grad_combine = found.reshape(top, tok_count).T
    shape_out = (exp_local, piece, most, source_count)
    return (
        gate_grad.reshape(shape_out).transpose(0, 3, 2, 1),
        up_grad.reshape(shape_out).transpose(0, 3, 2, 1),
        first_grad,
        second_grad,
        grad_combine,
    )


def solution(mesh):
    exp_width, seq_width = mesh.shape["exp"], mesh.shape["seq"]
    split = Mesh(mesh.devices.reshape(exp_width, seq_width // 2, 2), ("exp", "z", "core"))
    seq = ("z", "core")
    placed = (
        P("exp", seq),
        P("exp", None),
        P("exp", None),
        P("exp"),
        P("exp", None, None, seq),
        P("exp", None, None, seq),
        P("exp", None, seq),
        P("exp", None, seq, None),
        P("exp", None, None, seq),
    )
    return jax.shard_map(
        on_device,
        mesh=split,
        in_specs=placed,
        out_specs=(
            P("exp", None, None, seq),
            P("exp", None, None, seq),
            P("exp", None, seq, None),
            P("exp", None, None, seq),
            P("exp", None),
        ),
        check_vma=False,
    )
```
